128 devices in a mesh: ctx: 32 (over z, x, core), head: 4 (over y).
Axes of the slice: x: 4, y: 4, z: 4, core: 2. Of those that a mesh axis runs over, the one named last changes fastest.
Arguments:
- tokens: bfloat16 [16384, 4096], P('ctx', 'head'), may hold values from -6 to 6
- pair_weight: bfloat16 [4096, 256], replicated, may hold values from -0.09375 to 0.09375
- value_weight: bfloat16 [4096, 4096], P(None, 'head'), may hold values from -0.09375 to 0.09375
- output_weight: bfloat16 [4096, 4096], P('head'), may hold values from -0.09375 to 0.09375
- level_index: int32 [16384, 8], P('ctx'), may hold values from 0 to 15
- level_table: float32 [8, 16, 32], P(None, None, 'head'), may hold values from 0.05 to 1
- out_gain: float32 [4096], P('head'), may hold values from 0.5 to 1.5
Outputs:
- layer_out: bfloat16 [16384, 4096], P('ctx', 'head')
The draws below stay inside these ranges and needn't reach their ends.
All inputs are finite; a program needn't handle non-finite values.
Results may differ from the reference program's by a relative error of at most 0.02.
Values may be sent and summed in bfloat16 or wider, within the bound.
A program may use at most 128 MiB of HBM per device.

```python
import math
import jax
import jax.numpy as jnp
from jax import lax

D = 4096
HEADS = 32
DH = 128
DK = 128
SPAN = 128
NTAB = 16
TOKENS = 16384
HV = 4096
LOCAL_BITS = 2
CTX_BITS = 5
LEVELS = 8
N_HEAD = 4


def place_ends(values, stream_key, low, largest):
    longest = values.shape.index(max(values.shape))
    spots = []
    for shift in (0, 1):
        where = [jax.random.randint(jax.random.fold_in(stream_key, axis), (), 0, length) for axis, length in enumerate(values.shape)]
        where[longest] = (where[longest] + shift) % values.shape[longest]
        spots.append(tuple(where))
    return values.at[spots[0]].set(low).at[spots[1]].set(largest)


def block_scale(rng, extent, split, smallest, top_value):
    level, own = 1.0, jax.random.fold_in(rng, 6)
    for position, blocks in split:
        draws = jnp.exp(jax.random.uniform(jax.random.fold_in(own, position), (blocks,), jnp.float32, smallest / len(split), top_value / len(split)))
        level = level * jnp.repeat(draws, extent[position] // blocks).reshape([-1 if axis == position else 1 for axis in range(len(extent))])
    return level


def normal_values(stream_key, shape, scale, most, split=(), held_as=jnp.bfloat16):
    factor_of = block_scale(stream_key, shape, split, -0.22, 0.18) if split else 1.0
    drawn = jax.random.normal(stream_key, shape, jnp.float32) * scale * factor_of
    return jnp.minimum(jnp.maximum(drawn, -most), most).astype(held_as)


def setup_inputs(seed: int = 0) -> dict:
    streams_of = jax.random.split(jax.random.key(seed), 8)
    tokens = normal_values(streams_of[0], (TOKENS, D), 1.0, 6.0, ((0, 32), (1, 4)))
    pair_weight = normal_values(streams_of[1], (D, 2 * DK), D ** -0.5, 0.09375)
    value_weight = normal_values(streams_of[2], (D, HV), D ** -0.5, 0.09375, ((1, 4),))
    output_weight = normal_values(streams_of[3], (HV, D), HV ** -0.5, 0.09375, ((0, 4),))
    level_index = place_ends(jax.random.randint(streams_of[4], (TOKENS, LEVELS), 0, NTAB), jax.random.fold_in(streams_of[4], 1), 0, NTAB - 1).astype(jnp.int32)
    level_table = jnp.clip(jnp.exp(math.log(1.0) - 2.9957323 * jax.random.uniform(streams_of[5], (LEVELS, NTAB, HEADS), jnp.float32) ** block_scale(streams_of[5], (LEVELS, NTAB, HEADS), ((2, 4),), -0.2, 0.2)), 0.05, 1.0)
    out_gain = jnp.clip(1.0 + 0.1 * jax.random.normal(streams_of[6], (HV,), jnp.float32), 0.5, 1.5)
    return dict(tokens=tokens, pair_weight=pair_weight, value_weight=value_weight, output_weight=output_weight, level_index=level_index, level_table=level_table, out_gain=out_gain)


EPS = 1e-06

def rounded(values):
    return lax.optimization_barrier(values.astype(jnp.bfloat16)).astype(jnp.float32)

def unit_rows(values):
    scale = lax.rsqrt(lax.optimization_barrier(jnp.mean(values * values, axis=-1, keepdims=True)) + EPS)
    return values * scale / math.sqrt(values.shape[-1])

def reference(tokens, pair_weight, value_weight, output_weight, level_index, level_table, out_gain):
    token_count = TOKENS
    spans = token_count // SPAN
    paired = jnp.dot(tokens, pair_weight, preferred_element_type=jnp.float32)
    queries = rounded(unit_rows(paired[:, :DK]))
    keys_all = rounded(unit_rows(paired[:, DK:]))
    values = rounded(jnp.dot(tokens, value_weight, preferred_element_type=jnp.float32))
    level_ids = jnp.arange(LEVELS, dtype=jnp.int32)
    mixing = level_table[level_ids[None, :], level_index]
    query_blocks = queries.reshape(spans, SPAN, DK)
    key_blocks = keys_all.reshape(spans, SPAN, DK)
    scores = jnp.einsum('ncd,ned->nce', query_blocks, key_blocks)
    causal = jnp.arange(SPAN)[:, None] >= jnp.arange(SPAN)[None, :]
    scores = rounded(jnp.where(causal[None], scores, 0.0))
    span_ids = jnp.arange(spans, dtype=jnp.int32)
    head_values = values.reshape(token_count, HEADS, DH).transpose(1, 0, 2)
    head_mixing = mixing.transpose(2, 0, 1)

    def one_head(inputs):
        value_rows, weight_rows = inputs
        value_blocks = value_rows.reshape(spans, SPAN, DH)
        result = jnp.einsum('nce,nev->ncv', scores, value_blocks).reshape(token_count, DH)
        result = result * weight_rows[:, 0:1]
        states = jnp.einsum('ncd,ncv->ndv', key_blocks, value_blocks)
        for level_bit in range(LOCAL_BITS + CTX_BITS):
            block_width = 2 ** level_bit
            sums = states.reshape(spans // block_width, block_width, DK, DH).sum(axis=1)
            shifted = span_ids // block_width
            present = (shifted % 2).astype(jnp.float32)
            bucket = sums[jnp.maximum(shifted - 1, 0)] * present[:, None, None]
            bucket = rounded(bucket)
            readout = jnp.einsum('ncd,ndv->ncv', query_blocks, bucket).reshape(token_count, DH)
            result = result + weight_rows[:, level_bit + 1:level_bit + 2] * readout
        return result
    mixed = lax.map(one_head, (head_values, head_mixing)).transpose(1, 0, 2)
    normed = mixed * lax.rsqrt(lax.optimization_barrier(jnp.mean(mixed * mixed, axis=-1, keepdims=True)) + EPS)
    normed = normed * out_gain.reshape(HEADS, DH)
    hidden = normed.reshape(token_count, HEADS * DH).astype(jnp.bfloat16)
    group_width = HEADS * DH // N_HEAD
    accumulated = jnp.zeros((token_count, D), jnp.float32)
    for group_index in range(N_HEAD):
        lower_end = group_index * group_width
        partial_value = jnp.dot(hidden[:, lower_end:lower_end + group_width], output_weight[lower_end:lower_end + group_width], preferred_element_type=jnp.float32)
        accumulated = accumulated + rounded(partial_value)
    return accumulated.astype(jnp.bfloat16)
```

```python
import math

import jax
import jax.numpy as jnp
from jax import lax
from jax.experimental import pallas as pl
from jax.experimental.pallas import tpu as pltpu
from jax.sharding import PartitionSpec as P

DH = 128
DK = 128
SPAN = 128
EPS = 1e-06
CHUNKS = 4
WIDTH = 1024
TILE = 256
CHIPS = 16
MESH = pl.DeviceIdType.MESH
BF = jnp.bfloat16
F32 = jnp.float32


def dot(a, b):
    return jnp.dot(a, b, preferred_element_type=F32)


def unit_rows(values):
    scale = lax.rsqrt(jnp.mean(values * values, axis=-1, keepdims=True) + EPS)
    return values * scale / math.sqrt(values.shape[-1])


def kernel(
    tok, pw, vw, ow, lidx, ltab, gain, out,
    full, wv, owv, acc, mixn, q, s01, s0b, s2b, tot, tb, tpeer, mixed,
    cb, r1, sb, r2, r2o, hid, popp, rpopp, psum, rpsum, pown,
    w_sem, own_send, own_recv, fwd_send, fwd_recv, core_sem, one_sem, two_sem, swap_sem,
    opp_send, opp_recv, plain_send, plain_recv, sum_send, sum_recv,
):
    me = lax.axis_index("head")
    ctx = lax.axis_index("ctx")
    right = lax.rem(me + 1, 4)
    left = lax.rem(me + 3, 4)
    opposite = lax.rem(me + 2, 4)
    core = lax.rem(ctx, 2)
    chip = lax.div(ctx, 2)
    other = ctx + 1 - 2 * core
    bits = [lax.rem(lax.div(chip, 1 << i), 2) for i in range(4)]
    count = bits[0] + bits[1] + bits[2] + bits[3]

    def remote(src, dst, send, recv, **axes):
        return pltpu.make_async_remote_copy(
            src_ref=src, dst_ref=dst, send_sem=send, recv_sem=recv,
            device_id=axes, device_id_type=MESH,
        )

    loads = [
        pltpu.make_async_copy(pw, wv.at[4], w_sem.at[4]),
    ]
    for n in range(4):
        loads.append(pltpu.make_async_copy(vw.at[:, pl.ds(n * TILE, TILE)], wv.at[n], w_sem.at[n]))
    tok_load = pltpu.make_async_copy(tok, full.at[me], w_sem.at[5])
    ow_loads = [
        pltpu.make_async_copy(ow.at[:, pl.ds(t * TILE, TILE)], owv.at[t], w_sem.at[6 + t])
        for t in range(16)
    ]

    barrier = pltpu.get_barrier_semaphore()
    for peer in (left, right):
        pl.semaphore_signal(barrier, inc=1, device_id={"head": peer}, device_id_type=MESH)
    pl.semaphore_signal(barrier, inc=1, device_id={"ctx": other}, device_id_type=MESH)

    def greet(d, carry):
        dest = lax.rem(chip + d, CHIPS) * 2 + core
        pl.semaphore_signal(barrier, inc=1, device_id={"ctx": dest}, device_id_type=MESH)
        return carry

    lax.fori_loop(1, CHIPS, greet, 0)
    tok_load.start()
    for load in loads:
        load.start()
    pl.semaphore_wait(barrier, 3 + CHIPS - 1)

    peers = (right, left)
    HALF = SPAN // 2

    def own(r, d):
        rows = pl.ds(r * SPAN, SPAN)
        return remote(tok.at[rows], full.at[me, rows], own_send.at[d, r], own_recv.at[d, r], head=peers[d])

    def own_in(r, d):
        rows = pl.ds(r * SPAN, SPAN)
        slot = (left, right)[d]
        return remote(tok.at[rows], full.at[slot, rows], own_send.at[d, r], own_recv.at[d, r], head=peers[d])

    def forward(r, d):
        rows = pl.ds(r * SPAN + d * HALF, HALF)
        slot = (left, right)[d]
        return remote(full.at[slot, rows], full.at[slot, rows], fwd_send.at[d, r], fwd_recv.at[d, r], head=peers[d])

    def forward_in(r, d):
        rows = pl.ds(r * SPAN + d * HALF, HALF)
        return remote(full.at[opposite, rows], full.at[opposite, rows], fwd_send.at[d, r], fwd_recv.at[d, r], head=peers[d])

    for r in range(2):
        for d in range(2):
            own(r, d).start()

    level_of = lax.broadcasted_iota(jnp.int32, (8, 128), 0)
    lane = lax.broadcasted_iota(jnp.int32, (8, 128), 1)
    spread = jnp.where(level_of == lane // 16, 1.0, 0.0).astype(BF)
    wanted = dot(lidx[...].astype(F32).astype(BF), spread)
    entry = lax.broadcasted_iota(jnp.int32, (CHUNKS * SPAN, 128), 1) % 16
    onehot = jnp.where(wanted == entry.astype(F32), 1.0, 0.0)
    row = lax.broadcasted_iota(jnp.int32, (128, 128), 0)
    column = lax.broadcasted_iota(jnp.int32, (128, 128), 1)
    for n in range(4):
        first = jnp.broadcast_to(ltab[:, 2 * n : 2 * n + 1], (128, 128))
        second = jnp.broadcast_to(ltab[:, 2 * n + 1 : 2 * n + 2], (128, 128))
        table = jnp.where(row // 16 == column // 2, jnp.where(column % 2 == 0, first, second), 0.0)
        mixn[n] = jnp.dot(onehot, table, preferred_element_type=F32, precision=lax.Precision.HIGHEST)
    r2[4] = jnp.zeros((CHIPS, 16, TILE), BF)
    r2o[4] = jnp.zeros((CHIPS, 16, TILE), BF)

    def weighted(value, n, rows, level):
        parts = []
        for h in range(2):
            w = mixn[n, rows, 2 * level + h : 2 * level + h + 1]
            parts.append(value[:, h * DH : (h + 1) * DH] * w)
        return jnp.concatenate(parts, axis=1)

    for load in loads:
        load.wait()
    tok_load.wait()
    for load in ow_loads:
        load.start()

    def first_part(r):
        rows = pl.ds(r * SPAN, SPAN)

        def body(n, carry):
            total = None
            for slot in (me, left, right):
                term = dot(full[slot, rows, :], wv[n, pl.ds(pl.multiple_of(slot * WIDTH, WIDTH), WIDTH), :])
                total = term if total is None else total + term
            acc[r % 2, n] = total
            return carry

        lax.fori_loop(0, 5, body, 0)

    def second_part(r):
        rows = pl.ds(r * SPAN, SPAN)
        where = pl.ds(pl.multiple_of(opposite * WIDTH, WIDTH), WIDTH)
        block = full[opposite, rows, :]
        paired = acc[r % 2, 4] + dot(block, wv[4, where, :])
        query = unit_rows(paired[:, :DK]).astype(BF)
        key_t = unit_rows(paired[:, DK:]).T.astype(BF)
        q[rows, :] = query
        scores = dot(query, key_t)
        t = lax.broadcasted_iota(jnp.int32, (SPAN, SPAN), 0)
        s = lax.broadcasted_iota(jnp.int32, (SPAN, SPAN), 1)
        scores = jnp.where(t >= s, scores, 0.0).astype(BF)

        def body(n, carry):
            value = (acc[r % 2, n] + dot(full[opposite, rows, :], wv[n, where, :])).astype(BF)
            result = weighted(dot(scores, value), n, rows, 0)
            state = dot(key_t, value)
            if r == 0:
                s01[n] = state
                s0b[n] = state.astype(BF)
            elif r == 1:
                result += weighted(dot(query, s0b[n]), n, rows, 1)
                s01[n] = s01[n] + state
            elif r == 2:
                result += weighted(dot(query, s01[n].astype(BF)), n, rows, 2)
                s2b[n] = state.astype(BF)
                tot[n] = s01[n] + state
            else:
                result += weighted(dot(query, s2b[n]), n, rows, 1)
                result += weighted(dot(query, s01[n].astype(BF)), n, rows, 2)
                total = tot[n] + state
                tot[n] = total
                tb[n] = total.astype(BF)
            mixed[n, rows, :] = result
            return carry

        lax.fori_loop(0, 4, body, 0)

    for r in range(CHUNKS):
        for d in range(2):
            own_in(r, d).wait_recv()
            forward(r, d).start()
        if r + 2 < CHUNKS:
            for d in range(2):
                own(r + 2, d).start()
        first_part(r)
        if r > 0:
            for d in range(2):
                forward_in(r - 1, d).wait_recv()
            second_part(r - 1)
    for d in range(2):
        forward_in(CHUNKS - 1, d).wait_recv()
    second_part(CHUNKS - 1)

    core_copy = remote(tb, tpeer, core_sem.at[0], core_sem.at[1], ctx=other)
    core_copy.start()
    core_copy.wait_recv()
    for m in range(2):
        n = 2 * core + m
        both = tot[n] + tpeer[n].astype(F32)
        cb[m * 8 : (m + 1) * 8] = both.astype(BF).reshape(8, 16, TILE)

    def piece(d, carry):
        dest = lax.rem(chip + d, CHIPS)
        remote(cb.at[dest], r1.at[chip], one_sem.at[0], one_sem.at[1], ctx=dest * 2 + core).start()
        return carry

    lax.fori_loop(1, CHIPS, piece, 0)
    r1[chip] = cb[chip]
    others = pl.ds(0, CHIPS - 1)
    remote(cb.at[others], r1.at[others], one_sem.at[0], one_sem.at[1], ctx=other).wait_recv()

    piece_of = [r1[c].astype(F32) for c in range(CHIPS)]
    pair = [piece_of[4 * z] + piece_of[4 * z + 1] for z in range(4)]
    line = [pair[z] + (piece_of[4 * z + 2] + piece_of[4 * z + 3]) for z in range(4)]
    lower = line[0] + line[1]
    for c in range(CHIPS):
        z, x = c // 4, c % 4
        slot = 0
        for bit, value in ((x & 1, piece_of[c - 1]), (x & 2, pair[z]), (z & 1, line[z - 1]), (z & 2, lower)):
            if bit:
                sb[4 * c + slot] = value.astype(BF)
                slot += 1

    def spread_sums(d, carry):
        dest = lax.rem(chip + d, CHIPS)
        dest_count = sum(lax.rem(lax.div(dest, 1 << i), 2) for i in range(4))
        for j in range(1, 5):
            @pl.when(dest_count == j)
            def _():
                remote(
                    sb.at[pl.ds(4 * dest, j)], r2.at[pl.ds(0, j), chip],
                    two_sem.at[0], two_sem.at[1], ctx=dest * 2 + core,
                ).start()
        return carry

    lax.fori_loop(1, CHIPS, spread_sums, 0)
    for j in range(1, 5):
        @pl.when(count == j)
        def _():
            for s in range(j):
                r2[s, chip] = sb[4 * chip + s]
            here = r2.at[pl.ds(0, j), pl.ds(0, CHIPS - 1)]
            remote(here, here, two_sem.at[0], two_sem.at[1], ctx=other).wait_recv()
            remote(r2.at[pl.ds(0, j)], r2o.at[pl.ds(0, j)], swap_sem.at[0], swap_sem.at[1], ctx=other).start()

    rank = 0
    slots = []
    for i in range(4):
        slots.append(bits[i] * rank + (1 - bits[i]) * 4)
        rank = rank + bits[i]
    core_on = core.astype(F32)

    def far_tile(r, n, m, source):
        rows = pl.ds(r * SPAN, SPAN)
        query = q[rows, :]
        x = mixed[n, rows, :]
        x += weighted(dot(query, tpeer[n]) * core_on, n, rows, 3)
        for i in range(4):
            bucket = source[slots[i], pl.ds(pl.multiple_of(m * 8, 8), 8)].reshape(128, TILE)
            x += weighted(dot(query, bucket), n, rows, 4 + i)
        for h in range(2):
            one = x[:, h * DH : (h + 1) * DH]
            one = one * lax.rsqrt(jnp.mean(one * one, axis=-1, keepdims=True) + EPS)
            one = one * gain[2 * n + h]
            hid[rows, pl.ds(pl.multiple_of(n * TILE + h * DH, DH), DH)] = one.astype(BF)

    def far(r):
        def near_half(m, carry):
            far_tile(r, 2 * core + m, m, r2)
            return carry

        def far_half(m, carry):
            far_tile(r, 2 - 2 * core + m, m, r2o)
            return carry

        lax.fori_loop(0, 2, near_half, 0)
        if r == 0:
            for j in range(1, 5):
                @pl.when(count == j)
                def _():
                    copy = remote(r2.at[pl.ds(0, j)], r2o.at[pl.ds(0, j)], swap_sem.at[0], swap_sem.at[1], ctx=other)
                    copy.wait_recv()
        lax.fori_loop(0, 2, far_half, 0)

    def opp_copy(r, d):
        return remote(popp.at[r, d], rpopp.at[r, d], opp_send.at[d, r], opp_recv.at[d, r], head=peers[d])

    def plain_copy(r, d):
        half = pl.ds(2 - 2 * d, 2)
        return remote(psum.at[r, d, half], rpsum.at[r, d, half], plain_send.at[d, r], plain_recv.at[d, r], head=peers[d])

    def sum_copy(r, d):
        half = pl.ds(2 * d, 2)
        return remote(psum.at[r, d, half], rpsum.at[r, d, half], sum_send.at[d, r], sum_recv.at[d, r], head=peers[d])

    def project(r, dest, n):
        return dot(hid[pl.ds(r * SPAN, SPAN), :], owv[dest * 4 + n])

    def opposite_part(r):
        def body(n, carry):
            popp[r, lax.div(n, 2), lax.rem(n, 2)] = project(r, opposite, n).astype(BF)
            return carry

        lax.fori_loop(0, 4, body, 0)
        for d in range(2):
            opp_copy(r, d).start()

    def neighbour_part(r):
        for d in range(2):
            def body(n, carry):
                psum[r, d, n] = project(r, peers[d], n).astype(BF)
                return carry

            lax.fori_loop(0, 4, body, 0)
            plain_copy(r, d).start()

    def relay(r):
        for d in range(2):
            opp_copy(r, d).wait_recv()
            for m in range(2):
                n = 2 * d + m
                psum[r, d, n] = (psum[r, d, n].astype(F32) + rpopp[r, d, m].astype(F32)).astype(BF)
            sum_copy(r, d).start()

    def own_part(r):
        def body(n, carry):
            pown[r, n] = project(r, me, n).astype(BF)
            return carry

        lax.fori_loop(0, 4, body, 0)

    def finish(r):
        for d in range(2):
            plain_copy(r, d).wait_recv()
            sum_copy(r, d).wait_recv()
        for n in range(4):
            total = pown[r, n].astype(F32) + rpsum[r, 0, n].astype(F32) + rpsum[r, 1, n].astype(F32)
            out[pl.ds(r * SPAN, SPAN), n * TILE : (n + 1) * TILE] = total.astype(BF)

    for r in range(CHUNKS):
        far(r)
        if r == 0:
            for load in ow_loads:
                load.wait()
        opposite_part(r)
        if r > 0:
            relay(r - 1)
        neighbour_part(r)
        own_part(r)
    relay(CHUNKS - 1)
    for r in range(CHUNKS):
        finish(r)

    for r in range(CHUNKS):
        for d in range(2):
            own(r, d).wait_send()
            forward(r, d).wait_send()
            opp_copy(r, d).wait_send()
            plain_copy(r, d).wait_send()
            sum_copy(r, d).wait_send()
    core_copy.wait_send()
    remote(cb.at[others], r1.at[others], one_sem.at[0], one_sem.at[1], ctx=other).wait_send()
    for j in range(0, 5):
        @pl.when(count == j)
        def _():
            sent = sb.at[pl.ds(0, 32 - j)]
            remote(sent, sent, two_sem.at[0], two_sem.at[1], ctx=other).wait_send()
            if j:
                remote(r2.at[pl.ds(0, j)], r2o.at[pl.ds(0, j)], swap_sem.at[0], swap_sem.at[1], ctx=other).wait_send()


def local(tokens, pair_weight, value_weight, output_weight, level_index, level_table, out_gain):
    any_space = pl.BlockSpec(memory_space=pl.ANY)
    vmem = pl.BlockSpec(memory_space=pltpu.VMEM)
    rows = tokens.shape[0]
    dma = pltpu.SemaphoreType.DMA
    return pl.pallas_call(
        kernel,
        out_shape=jax.ShapeDtypeStruct((rows, WIDTH), BF),
        in_specs=[any_space] * 4 + [vmem] * 3,
        out_specs=vmem,
        scratch_shapes=[
            pltpu.VMEM((4, rows, WIDTH), BF),
            pltpu.VMEM((5, 4 * WIDTH, TILE), BF),
            pltpu.VMEM((16, WIDTH, TILE), BF),
            pltpu.VMEM((2, 5, SPAN, TILE), F32),
            pltpu.VMEM((4, rows, 128), F32),
            pltpu.VMEM((rows, DK), BF),
            pltpu.VMEM((4, DK, TILE), F32),
            pltpu.VMEM((4, DK, TILE), BF),
            pltpu.VMEM((4, DK, TILE), BF),
            pltpu.VMEM((4, DK, TILE), F32),
            pltpu.VMEM((4, DK, TILE), BF),
            pltpu.VMEM((4, DK, TILE), BF),
            pltpu.VMEM((4, rows, TILE), F32),
            pltpu.VMEM((CHIPS, 16, TILE), BF),
            pltpu.VMEM((CHIPS, 16, TILE), BF),
            pltpu.VMEM((4 * CHIPS, 16, TILE), BF),
            pltpu.VMEM((5, CHIPS, 16, TILE), BF),
            pltpu.VMEM((5, CHIPS, 16, TILE), BF),
            pltpu.VMEM((rows, WIDTH), BF),
            pltpu.VMEM((CHUNKS, 2, 2, SPAN, TILE), BF),
            pltpu.VMEM((CHUNKS, 2, 2, SPAN, TILE), BF),
            pltpu.VMEM((CHUNKS, 2, 4, SPAN, TILE), BF),
            pltpu.VMEM((CHUNKS, 2, 4, SPAN, TILE), BF),
            pltpu.VMEM((CHUNKS, 4, SPAN, TILE), BF),
            dma((22,)),
            dma((2, CHUNKS)),
            dma((2, CHUNKS)),
            dma((2, CHUNKS)),
            dma((2, CHUNKS)),
            dma((2,)),
            dma((2,)),
            dma((2,)),
            dma((2,)),
            dma((2, CHUNKS)),
            dma((2, CHUNKS)),
            dma((2, CHUNKS)),
            dma((2, CHUNKS)),
            dma((2, CHUNKS)),
            dma((2, CHUNKS)),
        ],
        compiler_params=pltpu.CompilerParams(
            collective_id=0, has_side_effects=True, vmem_limit_bytes=56 * 1024 * 1024
        ),
        name="layer",
    )(
        tokens, pair_weight, value_weight, output_weight, level_index,
        level_table.reshape(128, 8), out_gain.reshape(8, 1, 128),
    )


def solution(mesh):
    return jax.shard_map(
        local,
        mesh=mesh,
        in_specs=(
            P("ctx", "head"),
            P(),
            P(None, "head"),
            P("head", None),
            P("ctx", None),
            P(None, None, "head"),
            P("head"),
        ),
        out_specs=P("ctx", "head"),
        check_vma=False,
    )
```

```python
import math

import jax
import jax.numpy as jnp
from jax import lax
from jax.experimental import pallas as pl
from jax.experimental.pallas import tpu as pltpu
from jax.sharding import PartitionSpec as P

DH = 128
DK = 128
SPAN = 128
EPS = 1e-06
CHUNKS = 4
WIDTH = 1024
TILE = 256
CHIPS = 16
MESH = pl.DeviceIdType.MESH
BF = jnp.bfloat16
F32 = jnp.float32


def dot(a, b):
    return jnp.dot(a, b, preferred_element_type=F32)


def unit_rows(values):
    scale = lax.rsqrt(jnp.mean(values * values, axis=-1, keepdims=True) + EPS)
    return values * scale / math.sqrt(values.shape[-1])


def kernel(
    tok, pw, vw, ow, lidx, ltab, gain, out,
    full, wv, owv, acc, mixn, q, kt, last, s01, s0b, s2b, tot, tb, tpeer, mixed,
    cb, r1, sb, r2, r2o, hid, popp, rpopp, psum, rpsum, pown, stage,
    w_sem, own_send, own_recv, fwd_send, fwd_recv, core_send, core_recv, one_sem, pair_sem, two_send, two_recv,
    swap_send, swap_recv, out_sem,
    opp_send, opp_recv, plain_send, plain_recv, sum_send, sum_recv,
):
    me = lax.axis_index("head")
    ctx = lax.axis_index("ctx")
    right = lax.rem(me + 1, 4)
    left = lax.rem(me + 3, 4)
    opposite = lax.rem(me + 2, 4)
    core = lax.rem(ctx, 2)
    chip = lax.div(ctx, 2)
    other = ctx + 1 - 2 * core
    bits = [lax.rem(lax.div(chip, 1 << i), 2) for i in range(4)]
    count = bits[1] + bits[2] + bits[3]

    def remote(src, dst, send, recv, **axes):
        return pltpu.make_async_remote_copy(
            src_ref=src, dst_ref=dst, send_sem=send, recv_sem=recv,
            device_id=axes, device_id_type=MESH,
        )

    loads = [
        pltpu.make_async_copy(pw, wv.at[4], w_sem.at[4]),
    ]
    for n in range(4):
        loads.append(pltpu.make_async_copy(vw.at[:, pl.ds(n * TILE, TILE)], wv.at[n], w_sem.at[n]))
    tok_load = pltpu.make_async_copy(tok, full.at[me], w_sem.at[5])
    ow_loads = [
        pltpu.make_async_copy(ow.at[:, pl.ds(t * TILE, TILE)], owv.at[t], w_sem.at[6 + t])
        for t in range(16)
    ]

    barrier = pltpu.get_barrier_semaphore()
    for peer in (left, right):
        pl.semaphore_signal(barrier, inc=1, device_id={"head": peer}, device_id_type=MESH)
    pl.semaphore_signal(barrier, inc=1, device_id={"ctx": other}, device_id_type=MESH)

    def greet(d, carry):
        dest = lax.rem(chip + d, CHIPS) * 2 + core
        pl.semaphore_signal(barrier, inc=1, device_id={"ctx": dest}, device_id_type=MESH)
        return carry

    lax.fori_loop(1, CHIPS, greet, 0)
    tok_load.start()
    for load in loads:
        load.start()
    pl.semaphore_wait(barrier, 3 + CHIPS - 1)

    peers = (right, left)
    HALF = SPAN // 2

    def own(r, d):
        rows = pl.ds(r * SPAN, SPAN)
        return remote(tok.at[rows], full.at[me, rows], own_send.at[d, r], own_recv.at[d, r], head=peers[d])

    def own_in(r, d):
        rows = pl.ds(r * SPAN, SPAN)
        slot = (left, right)[d]
        return remote(tok.at[rows], full.at[slot, rows], own_send.at[d, r], own_recv.at[d, r], head=peers[d])

    def forward(r, d):
        rows = pl.ds(r * SPAN + d * HALF, HALF)
        slot = (left, right)[d]
        return remote(full.at[slot, rows], full.at[slot, rows], fwd_send.at[d, r], fwd_recv.at[d, r], head=peers[d])

    def forward_in(r, d):
        rows = pl.ds(r * SPAN + d * HALF, HALF)
        return remote(full.at[opposite, rows], full.at[opposite, rows], fwd_send.at[d, r], fwd_recv.at[d, r], head=peers[d])

    for r in range(2):
        for d in range(2):
            own(r, d).start()

    row = lax.broadcasted_iota(jnp.int32, (128, 8), 0)
    spread = jnp.where(row // 16 == lax.broadcasted_iota(jnp.int32, (128, 8), 1), 1.0, 0.0).astype(BF)
    wanted = dot(spread, lidx[...].astype(F32).astype(BF))
    entry = lax.broadcasted_iota(jnp.int32, (128, CHUNKS * SPAN), 0) % 16
    onehot = jnp.where(wanted == entry.astype(F32), 1.0, 0.0).T
    exact = lax.Precision.HIGHEST
    level_of = lax.broadcasted_iota(jnp.int32, (64, 128), 0) // 8
    lane_level = lax.broadcasted_iota(jnp.int32, (64, 128), 1) // 16
    placed = jnp.where(level_of == lane_level, jnp.concatenate([ltab[...]] * 8, axis=1), 0.0)
    column = lax.broadcasted_iota(jnp.int32, (128, 64), 0)
    source = lax.broadcasted_iota(jnp.int32, (128, 64), 1)
    for n in range(4):
        take = jnp.where((column < 16) & (source == (column // 2) * 8 + 2 * n + column % 2), 1.0, 0.0)
        table = jnp.dot(take, placed, preferred_element_type=F32, precision=exact).T
        mixn[n] = jnp.dot(onehot, table, preferred_element_type=F32, precision=exact)
    r2[4] = jnp.zeros((CHIPS, 16, TILE), BF)
    r2o[4] = jnp.zeros((CHIPS, 16, TILE), BF)

    def weighted(value, n, rows, level):
        parts = []
        for h in range(2):
            w = mixn[n, rows, 2 * level + h : 2 * level + h + 1]
            parts.append(value[:, h * DH : (h + 1) * DH] * w)
        return jnp.concatenate(parts, axis=1)

    for load in loads:
        load.wait()
    tok_load.wait()
    for load in ow_loads:
        load.start()

    def first_part(r):
        rows = pl.ds(r * SPAN, SPAN)

        def body(n, carry):
            total = None
            for slot in (me, left, right):
                term = dot(full[slot, rows, :], wv[n, pl.ds(pl.multiple_of(slot * WIDTH, WIDTH), WIDTH), :])
                total = term if total is None else total + term
            acc[r % 2, n] = total
            return carry

        lax.fori_loop(0, 5, body, 0)

    def heads_of(r):
        where = pl.ds(pl.multiple_of(opposite * WIDTH, WIDTH), WIDTH)
        rows = pl.ds(r * SPAN, SPAN)
        paired = acc[r % 2, 4] + dot(full[opposite, rows, :], wv[4, where, :])
        q[rows, :] = unit_rows(paired[:, :DK]).astype(BF)
        kt[...] = unit_rows(paired[:, DK:]).T.astype(BF)

    def value_of(r, n):
        where = pl.ds(pl.multiple_of(opposite * WIDTH, WIDTH), WIDTH)
        rows = pl.ds(r * SPAN, SPAN)
        return (acc[r % 2, n] + dot(full[opposite, rows, :], wv[n, where, :])).astype(BF)

    def score_of(r):
        scores = dot(q[pl.ds(r * SPAN, SPAN), :], kt[...])
        t = lax.broadcasted_iota(jnp.int32, (SPAN, SPAN), 0)
        s = lax.broadcasted_iota(jnp.int32, (SPAN, SPAN), 1)
        return jnp.where(t >= s, scores, 0.0).astype(BF)

    def near(r, n, scores, value):
        rows = pl.ds(r * SPAN, SPAN)
        query = q[rows, :]
        result = weighted(dot(scores, value), n, rows, 0)
        if r == 1:
            result += weighted(dot(query, s0b[n]), n, rows, 1)
        if r == 3:
            result += weighted(dot(query, s2b[n]), n, rows, 1)
        if r >= 2:
            result += weighted(dot(query, s01[n].astype(BF)), n, rows, 2)
        mixed[n, rows, :] = result

    def second_part(r):
        heads_of(r)
        scores = score_of(r)

        def body(n, carry):
            value = value_of(r, n)
            near(r, n, scores, value)
            state = dot(kt[...], value)
            if r == 0:
                s01[n] = state
                s0b[n] = state.astype(BF)
            elif r == 1:
                s01[n] = s01[n] + state
            else:
                s2b[n] = state.astype(BF)
                tot[n] = s01[n] + state
            return carry

        lax.fori_loop(0, 4, body, 0)

    for r in range(CHUNKS):
        for d in range(2):
            own_in(r, d).wait_recv()
            forward(r, d).start()
        if r + 2 < CHUNKS:
            for d in range(2):
                own(r + 2, d).start()
        first_part(r)
        if r > 0:
            for d in range(2):
                forward_in(r - 1, d).wait_recv()
            second_part(r - 1)
    for d in range(2):
        forward_in(CHUNKS - 1, d).wait_recv()

    def core_copy(n):
        return remote(tb.at[n], tpeer.at[n], core_send.at[n], core_recv.at[n], ctx=other)

    def piece(dest):
        return remote(cb.at[dest], r1.at[chip], one_sem.at[0], one_sem.at[1], ctx=dest * 2 + core)

    heads_of(3)
    for order in range(4):
        n = lax.rem(2 * (1 - core) + order, 4)
        value = value_of(3, n)
        last[n] = value
        total = tot[n] + dot(kt[...], value)
        tot[n] = total
        tb[n] = total.astype(BF)
        core_copy(n).start()
        if order >= 2:
            m = order - 2
            core_copy(n).wait_recv()
            both = tot[n] + tpeer[n].astype(F32)
            cb[m * 8 : (m + 1) * 8] = both.astype(BF).reshape(8, 16, TILE)

            def send_piece(d, carry):
                dest = m * 8 + lax.rem(chip + d, 8)

                @pl.when(dest != chip)
                def _():
                    piece(dest).start()

                return carry

            lax.fori_loop(0, 8, send_piece, 0)
    pair_copy = remote(cb, r2.at[0], pair_sem.at[0], pair_sem.at[1], ctx=lax.rem(ctx + 2, 32))

    @pl.when(bits[0] == 0)
    def _():
        pair_copy.start()

    r1[chip] = cb[chip]
    scores = score_of(3)

    def last_near(n, carry):
        near(3, n, scores, last[n])
        return carry

    lax.fori_loop(0, 4, last_near, 0)
    others = pl.ds(0, CHIPS - 1)
    remote(cb.at[others], r1.at[others], one_sem.at[0], one_sem.at[1], ctx=other).wait_recv()

    piece_of = [r1[c].astype(F32) for c in range(CHIPS)]
    pair = [piece_of[4 * z] + piece_of[4 * z + 1] for z in range(4)]
    line = [pair[z] + (piece_of[4 * z + 2] + piece_of[4 * z + 3]) for z in range(4)]
    lower = line[0] + line[1]
    for c in range(CHIPS):
        z, x = c // 4, c % 4
        slot = 0
        for bit, value in ((x & 2, pair[z]), (z & 1, line[z - 1]), (z & 2, lower)):
            if bit:
                sb[3 * c + slot] = value.astype(BF)
                slot += 1

    for s in range(1, 4):
        def send_sum(d, carry):
            dest = lax.rem(chip + d, CHIPS)
            dest_count = sum(lax.rem(lax.div(dest, 1 << i), 2) for i in range(1, 4))

            @pl.when(dest_count >= s)
            def _():
                remote(
                    sb.at[3 * dest + s - 1], r2.at[s, chip],
                    two_send, two_recv.at[s], ctx=dest * 2 + core,
                ).start()

            return carry

        lax.fori_loop(1, CHIPS, send_sum, 0)

    for n in range(2):
        core_copy(2 * (1 - core) + n).wait_recv()
    core_on = core.astype(F32)
    for r in range(CHUNKS):
        def core_level(n, carry):
            rows = pl.ds(r * SPAN, SPAN)
            mixed[n, rows, :] = mixed[n, rows, :] + weighted(dot(q[rows, :], tpeer[n]) * core_on, n, rows, 3)
            return carry

        lax.fori_loop(0, 4, core_level, 0)

    def swap(s):
        return remote(r2.at[s], r2o.at[s], swap_send.at[s], swap_recv.at[s], ctx=other)

    @pl.when(bits[0] == 1)
    def _():
        pair_copy.wait_recv()
        swap(0).start()

    for s in range(1, 4):
        @pl.when(count >= s)
        def _():
            r2[s, chip] = sb[3 * chip + s - 1]
            here = r2.at[s, others]
            remote(here, here, two_send, two_recv.at[s], ctx=other).wait_recv()
            swap(s).start()

    slots = [4 * (1 - bits[0])]
    rank = 1
    for i in range(1, 4):
        slots.append(bits[i] * rank + (1 - bits[i]) * 4)
        rank = rank + bits[i]

    def far_tile(r, n, m, source):
        rows = pl.ds(r * SPAN, SPAN)
        query = q[rows, :]
        x = mixed[n, rows, :]
        for i in range(4):
            bucket = source[slots[i], pl.ds(pl.multiple_of(m * 8, 8), 8)].reshape(128, TILE)
            x += weighted(dot(query, bucket), n, rows, 4 + i)
        for h in range(2):
            one = x[:, h * DH : (h + 1) * DH]
            one = one * lax.rsqrt(jnp.mean(one * one, axis=-1, keepdims=True) + EPS)
            one = one * gain[2 * n + h]
            hid[rows, pl.ds(pl.multiple_of(n * TILE + h * DH, DH), DH)] = one.astype(BF)

    def far(r):
        def near_half(m, carry):
            far_tile(r, 2 * core + m, m, r2)
            return carry

        def far_half(m, carry):
            far_tile(r, 2 - 2 * core + m, m, r2o)
            return carry

        lax.fori_loop(0, 2, near_half, 0)
        if r == 0:
            @pl.when(bits[0] == 1)
            def _():
                swap(0).wait_recv()

            for s in range(1, 4):
                @pl.when(count >= s)
                def _():
                    swap(s).wait_recv()

        lax.fori_loop(0, 2, far_half, 0)

    def opp_copy(r, d):
        return remote(popp.at[r, d], rpopp.at[r, d], opp_send.at[d, r], opp_recv.at[d, r], head=peers[d])

    def plain_copy(r, d):
        half = pl.ds(2 - 2 * d, 2)
        return remote(psum.at[r, d, half], rpsum.at[r, d, half], plain_send.at[d, r], plain_recv.at[d, r], head=peers[d])

    def sum_copy(r, d):
        half = pl.ds(2 * d, 2)
        return remote(psum.at[r, d, half], rpsum.at[r, d, half], sum_send.at[d, r], sum_recv.at[d, r], head=peers[d])

    def project(r, dest, n):
        return dot(hid[pl.ds(r * SPAN, SPAN), :], owv[dest * 4 + n])

    def opposite_part(r):
        def body(n, carry):
            popp[r, lax.div(n, 2), lax.rem(n, 2)] = project(r, opposite, n).astype(BF)
            return carry

        lax.fori_loop(0, 4, body, 0)
        for d in range(2):
            opp_copy(r, d).start()

    def neighbour_part(r):
        for d in range(2):
            def body(n, carry):
                psum[r, d, n] = project(r, peers[d], n).astype(BF)
                return carry

            lax.fori_loop(0, 4, body, 0)
            plain_copy(r, d).start()

    def relay(r):
        for d in range(2):
            opp_copy(r, d).wait_recv()
            for m in range(2):
                n = 2 * d + m
                psum[r, d, n] = (psum[r, d, n].astype(F32) + rpopp[r, d, m].astype(F32)).astype(BF)
            sum_copy(r, d).start()

    def own_part(r):
        def body(n, carry):
            pown[r, n] = project(r, me, n).astype(BF)
            return carry

        lax.fori_loop(0, 4, body, 0)

    def store(r):
        rows = pl.ds(r * SPAN, SPAN)
        return pltpu.make_async_copy(stage.at[rows], out.at[rows], out_sem.at[r])

    def finish(r):
        for d in range(2):
            plain_copy(r, d).wait_recv()
            sum_copy(r, d).wait_recv()
        for n in range(4):
            total = pown[r, n].astype(F32) + rpsum[r, 0, n].astype(F32) + rpsum[r, 1, n].astype(F32)
            stage[pl.ds(r * SPAN, SPAN), n * TILE : (n + 1) * TILE] = total.astype(BF)
        store(r).start()

    for r in range(CHUNKS):
        far(r)
        if r == 0:
            for load in ow_loads:
                load.wait()
        opposite_part(r)
        if r > 0:
            relay(r - 1)
        neighbour_part(r)
        own_part(r)
        if r > 1:
            finish(r - 2)
    relay(CHUNKS - 1)
    for r in range(CHUNKS - 2, CHUNKS):
        finish(r)

    for r in range(CHUNKS):
        for d in range(2):
            own(r, d).wait_send()
            forward(r, d).wait_send()
            opp_copy(r, d).wait_send()
            plain_copy(r, d).wait_send()
            sum_copy(r, d).wait_send()
    for r in range(CHUNKS):
        store(r).wait()
    for n in range(4):
        core_copy(n).wait_send()
    remote(cb.at[others], r1.at[others], one_sem.at[0], one_sem.at[1], ctx=other).wait_send()

    @pl.when(bits[0] == 0)
    def _():
        pair_copy.wait_send()

    @pl.when(bits[0] == 1)
    def _():
        swap(0).wait_send()

    for j in range(4):
        @pl.when(count == j)
        def _():
            sent = sb.at[pl.ds(0, 24 - j)]
            remote(sent, sent, two_send, two_recv.at[1], ctx=other).wait_send()
            for s in range(1, j + 1):
                swap(s).wait_send()


def local(tokens, pair_weight, value_weight, output_weight, level_index, level_table, out_gain):
    any_space = pl.BlockSpec(memory_space=pl.ANY)
    vmem = pl.BlockSpec(memory_space=pltpu.VMEM)
    rows = tokens.shape[0]
    dma = pltpu.SemaphoreType.DMA
    return pl.pallas_call(
        kernel,
        out_shape=jax.ShapeDtypeStruct((rows, WIDTH), BF),
        in_specs=[any_space] * 4 + [vmem] * 3,
        out_specs=any_space,
        scratch_shapes=[
            pltpu.VMEM((4, rows, WIDTH), BF),
            pltpu.VMEM((5, 4 * WIDTH, TILE), BF),
            pltpu.VMEM((16, WIDTH, TILE), BF),
            pltpu.VMEM((2, 5, SPAN, TILE), F32),
            pltpu.VMEM((4, rows, 128), F32),
            pltpu.VMEM((rows, DK), BF),
            pltpu.VMEM((DK, SPAN), BF),
            pltpu.VMEM((4, SPAN, TILE), BF),
            pltpu.VMEM((4, DK, TILE), F32),
            pltpu.VMEM((4, DK, TILE), BF),
            pltpu.VMEM((4, DK, TILE), BF),
            pltpu.VMEM((4, DK, TILE), F32),
            pltpu.VMEM((4, DK, TILE), BF),
            pltpu.VMEM((4, DK, TILE), BF),
            pltpu.VMEM((4, rows, TILE), F32),
            pltpu.VMEM((CHIPS, 16, TILE), BF),
            pltpu.VMEM((CHIPS, 16, TILE), BF),
            pltpu.VMEM((3 * CHIPS, 16, TILE), BF),
            pltpu.VMEM((5, CHIPS, 16, TILE), BF),
            pltpu.VMEM((5, CHIPS, 16, TILE), BF),
            pltpu.VMEM((rows, WIDTH), BF),
            pltpu.VMEM((CHUNKS, 2, 2, SPAN, TILE), BF),
            pltpu.VMEM((CHUNKS, 2, 2, SPAN, TILE), BF),
            pltpu.VMEM((CHUNKS, 2, 4, SPAN, TILE), BF),
            pltpu.VMEM((CHUNKS, 2, 4, SPAN, TILE), BF),
            pltpu.VMEM((CHUNKS, 4, SPAN, TILE), BF),
            pltpu.VMEM((rows, WIDTH), BF),
            dma((22,)),
            dma((2, CHUNKS)),
            dma((2, CHUNKS)),
            dma((2, CHUNKS)),
            dma((2, CHUNKS)),
            dma((4,)),
            dma((4,)),
            dma((2,)),
            dma((2,)),
            dma(()),
            dma((4,)),
            dma((4,)),
            dma((4,)),
            dma((CHUNKS,)),
            dma((2, CHUNKS)),
            dma((2, CHUNKS)),
            dma((2, CHUNKS)),
            dma((2, CHUNKS)),
            dma((2, CHUNKS)),
            dma((2, CHUNKS)),
        ],
        compiler_params=pltpu.CompilerParams(
            collective_id=0, has_side_effects=True, vmem_limit_bytes=56 * 1024 * 1024
        ),
        name="layer",
    )(
        tokens, pair_weight, value_weight, output_weight, level_index.T,
        level_table.transpose(0, 2, 1).reshape(64, 16), out_gain.reshape(8, 1, 128),
    )


def solution(mesh):
    return jax.shard_map(
        local,
        mesh=mesh,
        in_specs=(
            P("ctx", "head"),
            P(),
            P(None, "head"),
            P("head", None),
            P("ctx", None),
            P(None, None, "head"),
            P("head"),
        ),
        out_specs=P("ctx", "head"),
        check_vma=False,
    )
```

```python
import math

import jax
import jax.numpy as jnp
from jax import lax
from jax.experimental import pallas as pl
from jax.experimental.pallas import tpu as pltpu
from jax.sharding import PartitionSpec as P

DH = 128
DK = 128
SPAN = 128
EPS = 1e-06
CHUNKS = 4
WIDTH = 1024
TILE = 256
CHIPS = 16
MESH = pl.DeviceIdType.MESH
BF = jnp.bfloat16
F32 = jnp.float32


def dot(a, b):
    return jnp.dot(a, b, preferred_element_type=F32)


def unit_rows(values):
    scale = lax.rsqrt(jnp.mean(values * values, axis=-1, keepdims=True) + EPS)
    return values * scale / math.sqrt(values.shape[-1])


def kernel(
    tok, pw, vw, ow, lidx, ltab, gain, out,
    full, wv, owv, acc, mixn, q, kt, last, s01, s0b, s2b, tot, tb, tpeer, mixed,
    cb, r1, sb, r2, r2o, hid, popp, rpopp, psum, rpsum, pown,
    w_sem, own_send, own_recv, fwd_send, fwd_recv, core_send, core_recv, one_sem, pair_sem, two_send, two_recv,
    swap_send, swap_recv,
    opp_send, opp_recv, plain_send, plain_recv, sum_send, sum_recv,
):
    me = lax.axis_index("head")
    ctx = lax.axis_index("ctx")
    right = lax.rem(me + 1, 4)
    left = lax.rem(me + 3, 4)
    opposite = lax.rem(me + 2, 4)
    core = lax.rem(ctx, 2)
    chip = lax.div(ctx, 2)
    other = ctx + 1 - 2 * core
    bits = [lax.rem(lax.div(chip, 1 << i), 2) for i in range(4)]
    count = bits[1] + bits[2] + bits[3]
    z_of = [lax.rem(lax.div(chip, 4) + d, 4) for d in range(4)]
    x_of = [lax.rem(lax.rem(chip, 4) + d, 4) for d in range(4)]
    z_count = [lax.rem(z, 2) + lax.div(z, 2) for z in z_of]
    x_count = [lax.div(x, 2) for x in x_of]
    ring = [(dz, dx) for dz in range(4) for dx in range(4) if dz or dx]

    def remote(src, dst, send, recv, **axes):
        return pltpu.make_async_remote_copy(
            src_ref=src, dst_ref=dst, send_sem=send, recv_sem=recv,
            device_id=axes, device_id_type=MESH,
        )

    loads = [
        pltpu.make_async_copy(pw, wv.at[4], w_sem.at[4]),
    ]
    for n in range(4):
        loads.append(pltpu.make_async_copy(vw.at[:, pl.ds(n * TILE, TILE)], wv.at[n], w_sem.at[n]))
    tok_load = pltpu.make_async_copy(tok, full.at[me], w_sem.at[5])
    ow_loads = [
        pltpu.make_async_copy(ow.at[:, pl.ds(t * TILE, TILE)], owv.at[t], w_sem.at[6 + t])
        for t in range(16)
    ]

    barrier = pltpu.get_barrier_semaphore()
    for peer in (left, right):
        pl.semaphore_signal(barrier, inc=1, device_id={"head": peer}, device_id_type=MESH)
    pl.semaphore_signal(barrier, inc=1, device_id={"ctx": other}, device_id_type=MESH)

    for dz, dx in ring:
        dest = (4 * z_of[dz] + x_of[dx]) * 2 + core
        pl.semaphore_signal(barrier, inc=1, device_id={"ctx": dest}, device_id_type=MESH)
    tok_load.start()
    for load in loads:
        load.start()
    pl.semaphore_wait(barrier, 3 + CHIPS - 1)

    peers = (right, left)
    HALF = SPAN // 2

    def own(r, d):
        rows = pl.ds(r * SPAN, SPAN)
        return remote(tok.at[rows], full.at[me, rows], own_send.at[d, r], own_recv.at[d, r], head=peers[d])

    def own_in(r, d):
        rows = pl.ds(r * SPAN, SPAN)
        slot = (left, right)[d]
        return remote(tok.at[rows], full.at[slot, rows], own_send.at[d, r], own_recv.at[d, r], head=peers[d])

    def forward(r, d):
        rows = pl.ds(r * SPAN + d * HALF, HALF)
        slot = (left, right)[d]
        return remote(full.at[slot, rows], full.at[slot, rows], fwd_send.at[d, r], fwd_recv.at[d, r], head=peers[d])

    def forward_in(r, d):
        rows = pl.ds(r * SPAN + d * HALF, HALF)
        return remote(full.at[opposite, rows], full.at[opposite, rows], fwd_send.at[d, r], fwd_recv.at[d, r], head=peers[d])

    for r in range(2):
        for d in range(2):
            own(r, d).start()

    row = lax.broadcasted_iota(jnp.int32, (128, 8), 0)
    spread = jnp.where(row // 16 == lax.broadcasted_iota(jnp.int32, (128, 8), 1), 1.0, 0.0).astype(BF)
    wanted = dot(spread, lidx[...].astype(F32).astype(BF))
    entry = lax.broadcasted_iota(jnp.int32, (128, CHUNKS * SPAN), 0) % 16
    onehot = jnp.where(wanted == entry.astype(F32), 1.0, 0.0).T
    exact = lax.Precision.HIGHEST
    level_of = lax.broadcasted_iota(jnp.int32, (64, 128), 0) // 8
    lane_level = lax.broadcasted_iota(jnp.int32, (64, 128), 1) // 16
    placed = jnp.where(level_of == lane_level, jnp.concatenate([ltab[...]] * 8, axis=1), 0.0)
    column = lax.broadcasted_iota(jnp.int32, (128, 64), 0)
    source = lax.broadcasted_iota(jnp.int32, (128, 64), 1)
    for n in range(4):
        take = jnp.where((column < 16) & (source == (column // 2) * 8 + 2 * n + column % 2), 1.0, 0.0)
        table = jnp.dot(take, placed, preferred_element_type=F32, precision=exact).T
        mixn[n] = jnp.dot(onehot, table, preferred_element_type=F32, precision=exact)
    r2[4] = jnp.zeros((CHIPS, 16, TILE), BF)
    r2o[4] = jnp.zeros((CHIPS, 16, TILE), BF)

    def weighted(value, n, rows, level):
        parts = []
        for h in range(2):
            w = mixn[n, rows, 2 * level + h : 2 * level + h + 1]
            parts.append(value[:, h * DH : (h + 1) * DH] * w)
        return jnp.concatenate(parts, axis=1)

    for load in loads:
        load.wait()
    tok_load.wait()
    for load in ow_loads:
        load.start()

    def first_part(r):
        rows = pl.ds(r * SPAN, SPAN)

        def body(n, carry):
            total = None
            for slot in (me, left, right):
                term = dot(full[slot, rows, :], wv[n, pl.ds(pl.multiple_of(slot * WIDTH, WIDTH), WIDTH), :])
                total = term if total is None else total + term
            acc[r % 2, n] = total
            return carry

        lax.fori_loop(0, 5, body, 0)

    def heads_of(r):
        where = pl.ds(pl.multiple_of(opposite * WIDTH, WIDTH), WIDTH)
        rows = pl.ds(r * SPAN, SPAN)
        paired = acc[r % 2, 4] + dot(full[opposite, rows, :], wv[4, where, :])
        q[rows, :] = unit_rows(paired[:, :DK]).astype(BF)
        kt[...] = unit_rows(paired[:, DK:]).T.astype(BF)

    def value_of(r, n):
        where = pl.ds(pl.multiple_of(opposite * WIDTH, WIDTH), WIDTH)
        rows = pl.ds(r * SPAN, SPAN)
        return (acc[r % 2, n] + dot(full[opposite, rows, :], wv[n, where, :])).astype(BF)

    def score_of(r):
        scores = dot(q[pl.ds(r * SPAN, SPAN), :], kt[...])
        t = lax.broadcasted_iota(jnp.int32, (SPAN, SPAN), 0)
        s = lax.broadcasted_iota(jnp.int32, (SPAN, SPAN), 1)
        return jnp.where(t >= s, scores, 0.0).astype(BF)

    def near(r, n, scores, value):
        rows = pl.ds(r * SPAN, SPAN)
        query = q[rows, :]
        result = weighted(dot(scores, value), n, rows, 0)
        if r == 1:
            result += weighted(dot(query, s0b[n]), n, rows, 1)
        if r == 3:
            result += weighted(dot(query, s2b[n]), n, rows, 1)
        if r >= 2:
            result += weighted(dot(query, s01[n].astype(BF)), n, rows, 2)
        mixed[n, rows, :] = result

    def second_part(r):
        heads_of(r)
        scores = score_of(r)

        def body(n, carry):
            value = value_of(r, n)
            near(r, n, scores, value)
            state = dot(kt[...], value)
            if r == 0:
                s01[n] = state
                s0b[n] = state.astype(BF)
            elif r == 1:
                s01[n] = s01[n] + state
            else:
                s2b[n] = state.astype(BF)
                tot[n] = s01[n] + state
            return carry

        lax.fori_loop(0, 4, body, 0)

    for r in range(CHUNKS):
        for d in range(2):
            own_in(r, d).wait_recv()
            forward(r, d).start()
        if r + 2 < CHUNKS:
            for d in range(2):
                own(r + 2, d).start()
        first_part(r)
        if r > 0:
            for d in range(2):
                forward_in(r - 1, d).wait_recv()
            second_part(r - 1)
    for d in range(2):
        forward_in(CHUNKS - 1, d).wait_recv()

    def core_copy(n):
        return remote(tb.at[n], tpeer.at[n], core_send.at[n], core_recv.at[n], ctx=other)

    def piece(dest):
        return remote(cb.at[dest], r1.at[chip], one_sem.at[0], one_sem.at[1], ctx=dest * 2 + core)

    end_rows = pl.ds(3 * SPAN, SPAN)
    end_where = pl.ds(pl.multiple_of(opposite * WIDTH, WIDTH), WIDTH)
    key = acc[1, 4, :, DK:] + dot(full[opposite, end_rows, :], wv[4, end_where, DK:])
    values = []
    for order in range(4):
        values.append(value_of(3, lax.rem(2 * (1 - core) + order, 4)))
    key_t = unit_rows(key).T.astype(BF)
    kt[...] = key_t
    for order in range(4):
        n = lax.rem(2 * (1 - core) + order, 4)
        last[n] = values[order]
        total = tot[n] + dot(key_t, values[order])
        tot[n] = total
        tb[n] = total.astype(BF)
        core_copy(n).start()
        if order >= 2:
            m = order - 2
            core_copy(n).wait_recv()
            both = tot[n] + tpeer[n].astype(F32)
            cb[m * 8 : (m + 1) * 8] = both.astype(BF).reshape(8, 16, TILE)

            for dz in range(2):
                z = 2 * m + lax.rem(z_of[0] + dz, 2)
                for dx in range(4):
                    dest = 4 * z + x_of[dx]
                    if dx:
                        piece(dest).start()
                    else:
                        @pl.when(dest != chip)
                        def _():
                            piece(dest).start()

    pair_copy = remote(cb, r2.at[0], pair_sem.at[0], pair_sem.at[1], ctx=lax.rem(ctx + 2, 32))

    @pl.when(bits[0] == 0)
    def _():
        pair_copy.start()

    r1[chip] = cb[chip]
    query = acc[1, 4, :, :DK] + dot(full[opposite, end_rows, :], wv[4, end_where, :DK])
    q[end_rows, :] = unit_rows(query).astype(BF)
    scores = score_of(3)

    def last_near(n, carry):
        near(3, n, scores, last[n])
        return carry

    lax.fori_loop(0, 4, last_near, 0)
    others = pl.ds(0, CHIPS - 1)
    remote(cb.at[others], r1.at[others], one_sem.at[0], one_sem.at[1], ctx=other).wait_recv()

    piece_of = [r1[c].astype(F32) for c in range(CHIPS)]
    pair = [piece_of[4 * z] + piece_of[4 * z + 1] for z in range(4)]
    line = [pair[z] + (piece_of[4 * z + 2] + piece_of[4 * z + 3]) for z in range(4)]
    lower = line[0] + line[1]
    for c in range(CHIPS):
        z, x = c // 4, c % 4
        slot = 0
        for bit, value in ((x & 2, pair[z]), (z & 1, line[z - 1]), (z & 2, lower)):
            if bit:
                sb[3 * c + slot] = value.astype(BF)
                slot += 1

    for s in range(1, 4):
        for dz, dx in ring:
            dest = 4 * z_of[dz] + x_of[dx]

            @pl.when(z_count[dz] + x_count[dx] >= s)
            def _():
                remote(
                    sb.at[3 * dest + s - 1], r2.at[s, chip],
                    two_send, two_recv.at[s], ctx=dest * 2 + core,
                ).start()


    for n in range(2):
        core_copy(2 * (1 - core) + n).wait_recv()
    core_on = core.astype(F32)
    def core_level(r):
        rows = pl.ds(r * SPAN, SPAN)
        def body(n, carry):
            mixed[n, rows, :] = mixed[n, rows, :] + weighted(dot(q[rows, :], tpeer[n]) * core_on, n, rows, 3)
            return carry

        lax.fori_loop(0, 4, body, 0)

    core_level(0)

    def swap(s):
        return remote(r2.at[s], r2o.at[s], swap_send.at[s], swap_recv.at[s], ctx=other)

    slots = [4 * (1 - bits[0])]
    rank = 1
    for i in range(1, 4):
        slots.append(bits[i] * rank + (1 - bits[i]) * 4)
        rank = rank + bits[i]

    def far_level(r, n, m, source, i):
        rows = pl.ds(r * SPAN, SPAN)
        bucket = source[slots[i], m * 8 : m * 8 + 8].reshape(128, TILE)
        return weighted(dot(q[rows, :], bucket), n, rows, 4 + i)

    def close(r, n, x):
        rows = pl.ds(r * SPAN, SPAN)
        for h in range(2):
            one = x[:, h * DH : (h + 1) * DH]
            one = one * lax.rsqrt(jnp.mean(one * one, axis=-1, keepdims=True) + EPS)
            one = one * gain[2 * n + h]
            hid[rows, pl.ds(pl.multiple_of(n * TILE + h * DH, DH), DH)] = one.astype(BF)

    first_rows = pl.ds(0, SPAN)
    for i in range(4):
        @pl.when(bits[i] == 1)
        def _():
            if i == 0:
                pair_copy.wait_recv()
            else:
                r2[slots[i], chip] = sb[3 * chip + slots[i] - 1]
                here = r2.at[slots[i], others]
                remote(here, here, two_send, two_recv.at[slots[i]], ctx=other).wait_recv()
            swap(slots[i]).start()

        for m in range(2):
            n = 2 * core + m
            x = mixed[n, first_rows, :] + far_level(0, n, m, r2, i)
            if i < 3:
                mixed[n, first_rows, :] = x
            else:
                close(0, n, x)
    for i in range(4):
        @pl.when(bits[i] == 1)
        def _():
            swap(slots[i]).wait_recv()

        for m in range(2):
            n = 2 - 2 * core + m
            x = mixed[n, first_rows, :] + far_level(0, n, m, r2o, i)
            if i < 3:
                mixed[n, first_rows, :] = x
            else:
                close(0, n, x)

    def far(r):
        core_level(r)
        rows = pl.ds(r * SPAN, SPAN)

        def body(m, carry):
            for n, source in ((2 * core + m, r2), (2 - 2 * core + m, r2o)):
                x = mixed[n, rows, :]
                for i in range(4):
                    bucket = source[slots[i], pl.ds(pl.multiple_of(m * 8, 8), 8)].reshape(128, TILE)
                    x += weighted(dot(q[rows, :], bucket), n, rows, 4 + i)
                close(r, n, x)
            return carry

        lax.fori_loop(0, 2, body, 0)

    def opp_copy(r, d):
        return remote(popp.at[r, d], rpopp.at[r, d], opp_send.at[d, r], opp_recv.at[d, r], head=peers[d])

    def plain_copy(r, d):
        half = pl.ds(2 - 2 * d, 2)
        return remote(psum.at[r, d, half], rpsum.at[r, d, half], plain_send.at[d, r], plain_recv.at[d, r], head=peers[d])

    def sum_copy(r, d):
        half = pl.ds(2 * d, 2)
        return remote(psum.at[r, d, half], rpsum.at[r, d, half], sum_send.at[d, r], sum_recv.at[d, r], head=peers[d])

    def project(r, dest, n):
        return dot(hid[pl.ds(r * SPAN, SPAN), :], owv[dest * 4 + n])

    def opposite_part(r):
        for d in range(2):
            def body(m, carry):
                popp[r, d, m] = project(r, opposite, 2 * d + m).astype(BF)
                return carry

            lax.fori_loop(0, 2, body, 0)
            opp_copy(r, d).start()

    def neighbour_part(r):
        for d in range(2):
            def body(n, carry):
                psum[r, d, n] = project(r, peers[d], n).astype(BF)
                return carry

            lax.fori_loop(0, 4, body, 0)
            plain_copy(r, d).start()

    def relay(r):
        for d in range(2):
            opp_copy(r, d).wait_recv()
            for m in range(2):
                n = 2 * d + m
                psum[r, d, n] = (psum[r, d, n].astype(F32) + rpopp[r, d, m].astype(F32)).astype(BF)
            sum_copy(r, d).start()

    def own_part(r):
        def body(n, carry):
            pown[r, n] = project(r, me, n).astype(BF)
            return carry

        lax.fori_loop(0, 4, body, 0)

    def finish(r):
        for d in range(2):
            plain_copy(r, d).wait_recv()
            sum_copy(r, d).wait_recv()
        for n in range(4):
            total = pown[r, n].astype(F32) + rpsum[r, 0, n].astype(F32) + rpsum[r, 1, n].astype(F32)
            out[pl.ds(r * SPAN, SPAN), n * TILE : (n + 1) * TILE] = total.astype(BF)

    for r in range(CHUNKS):
        if r > 0:
            far(r)
        if r == 0:
            for load in ow_loads:
                load.wait()
        opposite_part(r)
        neighbour_part(r)
        own_part(r)
        relay(r)
        if r > 1:
            finish(r - 2)
    for r in range(CHUNKS - 2, CHUNKS):
        finish(r)

    for r in range(CHUNKS):
        for d in range(2):
            own(r, d).wait_send()
            forward(r, d).wait_send()
            opp_copy(r, d).wait_send()
            plain_copy(r, d).wait_send()
            sum_copy(r, d).wait_send()
    for n in range(4):
        core_copy(n).wait_send()
    remote(cb.at[others], r1.at[others], one_sem.at[0], one_sem.at[1], ctx=other).wait_send()

    @pl.when(bits[0] == 0)
    def _():
        pair_copy.wait_send()

    @pl.when(bits[0] == 1)
    def _():
        swap(0).wait_send()

    for j in range(4):
        @pl.when(count == j)
        def _():
            sent = sb.at[pl.ds(0, 24 - j)]
            remote(sent, sent, two_send, two_recv.at[1], ctx=other).wait_send()
            for s in range(1, j + 1):
                swap(s).wait_send()


def local(tokens, pair_weight, value_weight, output_weight, level_index, level_table, out_gain):
    any_space = pl.BlockSpec(memory_space=pl.ANY)
    vmem = pl.BlockSpec(memory_space=pltpu.VMEM)
    rows = tokens.shape[0]
    dma = pltpu.SemaphoreType.DMA
    return pl.pallas_call(
        kernel,
        out_shape=pltpu.VMEM((rows, WIDTH), BF),
        in_specs=[any_space] * 4 + [vmem] * 3,
        out_specs=vmem,
        scratch_shapes=[
            pltpu.VMEM((4, rows, WIDTH), BF),
            pltpu.VMEM((5, 4 * WIDTH, TILE), BF),
            pltpu.VMEM((16, WIDTH, TILE), BF),
            pltpu.VMEM((2, 5, SPAN, TILE), F32),
            pltpu.VMEM((4, rows, 128), F32),
            pltpu.VMEM((rows, DK), BF),
            pltpu.VMEM((DK, SPAN), BF),
            pltpu.VMEM((4, SPAN, TILE), BF),
            pltpu.VMEM((4, DK, TILE), F32),
            pltpu.VMEM((4, DK, TILE), BF),
            pltpu.VMEM((4, DK, TILE), BF),
            pltpu.VMEM((4, DK, TILE), F32),
            pltpu.VMEM((4, DK, TILE), BF),
            pltpu.VMEM((4, DK, TILE), BF),
            pltpu.VMEM((4, rows, TILE), F32),
            pltpu.VMEM((CHIPS, 16, TILE), BF),
            pltpu.VMEM((CHIPS, 16, TILE), BF),
            pltpu.VMEM((3 * CHIPS, 16, TILE), BF),
            pltpu.VMEM((5, CHIPS, 16, TILE), BF),
            pltpu.VMEM((5, CHIPS, 16, TILE), BF),
            pltpu.VMEM((rows, WIDTH), BF),
            pltpu.VMEM((CHUNKS, 2, 2, SPAN, TILE), BF),
            pltpu.VMEM((CHUNKS, 2, 2, SPAN, TILE), BF),
            pltpu.VMEM((CHUNKS, 2, 4, SPAN, TILE), BF),
            pltpu.VMEM((CHUNKS, 2, 4, SPAN, TILE), BF),
            pltpu.VMEM((CHUNKS, 4, SPAN, TILE), BF),
            dma((22,)),
            dma((2, CHUNKS)),
            dma((2, CHUNKS)),
            dma((2, CHUNKS)),
            dma((2, CHUNKS)),
            dma((4,)),
            dma((4,)),
            dma((2,)),
            dma((2,)),
            dma(()),
            dma((4,)),
            dma((4,)),
            dma((4,)),
            dma((2, CHUNKS)),
            dma((2, CHUNKS)),
            dma((2, CHUNKS)),
            dma((2, CHUNKS)),
            dma((2, CHUNKS)),
            dma((2, CHUNKS)),
        ],
        compiler_params=pltpu.CompilerParams(
            collective_id=0, has_side_effects=True, vmem_limit_bytes=56 * 1024 * 1024
        ),
        name="layer",
    )(
        tokens, pair_weight, value_weight, output_weight, level_index.T,
        level_table.transpose(0, 2, 1).reshape(64, 16), out_gain.reshape(8, 1, 128),
    )


def solution(mesh):
    return jax.shard_map(
        local,
        mesh=mesh,
        in_specs=(
            P("ctx", "head"),
            P(),
            P(None, "head"),
            P("head", None),
            P("ctx", None),
            P(None, None, "head"),
            P("head"),
        ),
        out_specs=P("ctx", "head"),
        check_vma=False,
    )
```

```python
import math

import jax
import jax.numpy as jnp
from jax import lax
from jax.experimental import pallas as pl
from jax.experimental.pallas import tpu as pltpu
from jax.sharding import PartitionSpec as P

DH = 128
DK = 128
SPAN = 128
EPS = 1e-06
CHUNKS = 4
WIDTH = 1024
TILE = 256
CHIPS = 16
MESH = pl.DeviceIdType.MESH
BF = jnp.bfloat16
F32 = jnp.float32


def dot(a, b):
    return jnp.dot(a, b, preferred_element_type=F32)


def unit_rows(values):
    scale = lax.rsqrt(jnp.mean(values * values, axis=-1, keepdims=True) + EPS)
    return values * scale / math.sqrt(values.shape[-1])


def kernel(
    tok, pw, vw, ow, lidx_in, ltab_in, gain_in, out,
    lidx, ltab, gain,
    full, wv, owv, acc, mixn, q, kt, last, s01, s0b, s2b, tot, tb, tpeer, mixed,
    cb, r1, sb, r2, r2o, hid, popp, rpopp, psum, rpsum, pown,
    w_sem, own_send, own_recv, fwd_send, fwd_recv, core_send, core_recv, one_sem, pair_sem, two_send, two_recv,
    swap_send, swap_recv,
    opp_send, opp_recv, plain_send, plain_recv, sum_send, sum_recv,
):
    me = lax.axis_index("head")
    ctx = lax.axis_index("ctx")
    right = lax.rem(me + 1, 4)
    left = lax.rem(me + 3, 4)
    opposite = lax.rem(me + 2, 4)
    core = lax.rem(ctx, 2)
    chip = lax.div(ctx, 2)
    other = ctx + 1 - 2 * core
    bits = [lax.rem(lax.div(chip, 1 << i), 2) for i in range(4)]
    count = bits[1] + bits[2] + bits[3]
    z_of = [lax.rem(lax.div(chip, 4) + d, 4) for d in range(4)]
    x_of = [lax.rem(lax.rem(chip, 4) + d, 4) for d in range(4)]
    z_count = [lax.rem(z, 2) + lax.div(z, 2) for z in z_of]
    x_count = [lax.div(x, 2) for x in x_of]
    ring = [(dz, dx) for dz in range(4) for dx in range(4) if dz or dx]

    def remote(src, dst, send, recv, **axes):
        return pltpu.make_async_remote_copy(
            src_ref=src, dst_ref=dst, send_sem=send, recv_sem=recv,
            device_id=axes, device_id_type=MESH,
        )

    loads = [
        pltpu.make_async_copy(pw, wv.at[4], w_sem.at[4]),
    ]
    for n in range(4):
        loads.append(pltpu.make_async_copy(vw.at[:, pl.ds(n * TILE, TILE)], wv.at[n], w_sem.at[n]))
    tok_load = pltpu.make_async_copy(tok, full.at[me], w_sem.at[5])
    ow_loads = [
        pltpu.make_async_copy(ow.at[:, pl.ds(t * TILE, TILE)], owv.at[t], w_sem.at[6 + t])
        for t in range(16)
    ]

    barrier = pltpu.get_barrier_semaphore()
    for peer in (left, right):
        pl.semaphore_signal(barrier, inc=1, device_id={"head": peer}, device_id_type=MESH)
    pl.semaphore_signal(barrier, inc=1, device_id={"ctx": other}, device_id_type=MESH)

    for dz, dx in ring:
        dest = (4 * z_of[dz] + x_of[dx]) * 2 + core
        pl.semaphore_signal(barrier, inc=1, device_id={"ctx": dest}, device_id_type=MESH)
    small = [
        pltpu.make_async_copy(src, dst, w_sem.at[22 + i])
        for i, (src, dst) in enumerate(((lidx_in, lidx), (ltab_in, ltab), (gain_in, gain)))
    ]
    for load in small:
        load.start()
    tok_load.start()
    for load in loads:
        load.start()
    pl.semaphore_wait(barrier, 3 + CHIPS - 1)

    peers = (right, left)
    HALF = SPAN // 2

    def own(r, d):
        rows = pl.ds(r * SPAN, SPAN)
        return remote(tok.at[rows], full.at[me, rows], own_send.at[d, r], own_recv.at[d, r], head=peers[d])

    def own_in(r, d):
        rows = pl.ds(r * SPAN, SPAN)
        slot = (left, right)[d]
        return remote(tok.at[rows], full.at[slot, rows], own_send.at[d, r], own_recv.at[d, r], head=peers[d])

    def forward(r, d):
        rows = pl.ds(r * SPAN + d * HALF, HALF)
        slot = (left, right)[d]
        return remote(full.at[slot, rows], full.at[slot, rows], fwd_send.at[d, r], fwd_recv.at[d, r], head=peers[d])

    def forward_in(r, d):
        rows = pl.ds(r * SPAN + d * HALF, HALF)
        return remote(full.at[opposite, rows], full.at[opposite, rows], fwd_send.at[d, r], fwd_recv.at[d, r], head=peers[d])

    for r in range(2):
        for d in range(2):
            own(r, d).start()

    for load in small:
        load.wait()
    row = lax.broadcasted_iota(jnp.int32, (128, 8), 0)
    spread = jnp.where(row // 16 == lax.broadcasted_iota(jnp.int32, (128, 8), 1), 1.0, 0.0).astype(BF)
    wanted = dot(spread, lidx[...].astype(F32).astype(BF))
    entry = lax.broadcasted_iota(jnp.int32, (128, CHUNKS * SPAN), 0) % 16
    onehot = jnp.where(wanted == entry.astype(F32), 1.0, 0.0).T
    exact = lax.Precision.HIGHEST
    level_of = lax.broadcasted_iota(jnp.int32, (64, 128), 0) // 8
    lane_level = lax.broadcasted_iota(jnp.int32, (64, 128), 1) // 16
    placed = jnp.where(level_of == lane_level, jnp.concatenate([ltab[...]] * 8, axis=1), 0.0)
    column = lax.broadcasted_iota(jnp.int32, (128, 64), 0)
    source = lax.broadcasted_iota(jnp.int32, (128, 64), 1)
    for n in range(4):
        take = jnp.where((column < 16) & (source == (column // 2) * 8 + 2 * n + column % 2), 1.0, 0.0)
        table = jnp.dot(take, placed, preferred_element_type=F32, precision=exact).T
        mixn[n] = jnp.dot(onehot, table, preferred_element_type=F32, precision=exact)
    r2[4] = jnp.zeros((CHIPS, 16, TILE), BF)
    r2o[4] = jnp.zeros((CHIPS, 16, TILE), BF)

    def weighted(value, n, rows, level):
        parts = []
        for h in range(2):
            w = mixn[n, rows, 2 * level + h : 2 * level + h + 1]
            parts.append(value[:, h * DH : (h + 1) * DH] * w)
        return jnp.concatenate(parts, axis=1)

    for load in loads:
        load.wait()
    tok_load.wait()
    for load in ow_loads:
        load.start()

    def first_part(r):
        rows = pl.ds(r * SPAN, SPAN)

        def body(n, carry):
            total = None
            for slot in (me, left, right):
                term = dot(full[slot, rows, :], wv[n, pl.ds(pl.multiple_of(slot * WIDTH, WIDTH), WIDTH), :])
                total = term if total is None else total + term
            acc[r % 2, n] = total
            return carry

        lax.fori_loop(0, 5, body, 0)

    def heads_of(r):
        where = pl.ds(pl.multiple_of(opposite * WIDTH, WIDTH), WIDTH)
        rows = pl.ds(r * SPAN, SPAN)
        paired = acc[r % 2, 4] + dot(full[opposite, rows, :], wv[4, where, :])
        q[rows, :] = unit_rows(paired[:, :DK]).astype(BF)
        kt[...] = unit_rows(paired[:, DK:]).T.astype(BF)

    def value_of(r, n):
        where = pl.ds(pl.multiple_of(opposite * WIDTH, WIDTH), WIDTH)
        rows = pl.ds(r * SPAN, SPAN)
        return (acc[r % 2, n] + dot(full[opposite, rows, :], wv[n, where, :])).astype(BF)

    def score_of(r):
        scores = dot(q[pl.ds(r * SPAN, SPAN), :], kt[...])
        t = lax.broadcasted_iota(jnp.int32, (SPAN, SPAN), 0)
        s = lax.broadcasted_iota(jnp.int32, (SPAN, SPAN), 1)
        return jnp.where(t >= s, scores, 0.0).astype(BF)

    def near(r, n, scores, value):
        rows = pl.ds(r * SPAN, SPAN)
        query = q[rows, :]
        result = weighted(dot(scores, value), n, rows, 0)
        if r == 1:
            result += weighted(dot(query, s0b[n]), n, rows, 1)
        if r == 3:
            result += weighted(dot(query, s2b[n]), n, rows, 1)
        if r >= 2:
            result += weighted(dot(query, s01[n].astype(BF)), n, rows, 2)
        mixed[n, rows, :] = result

    def second_part(r):
        heads_of(r)
        scores = score_of(r)

        def body(n, carry):
            value = value_of(r, n)
            near(r, n, scores, value)
            state = dot(kt[...], value)
            if r == 0:
                s01[n] = state
                s0b[n] = state.astype(BF)
            elif r == 1:
                s01[n] = s01[n] + state
            else:
                s2b[n] = state.astype(BF)
                tot[n] = s01[n] + state
            return carry

        lax.fori_loop(0, 4, body, 0)

    for r in range(CHUNKS):
        for d in range(2):
            own_in(r, d).wait_recv()
            forward(r, d).start()
        if r + 2 < CHUNKS:
            for d in range(2):
                own(r + 2, d).start()
        first_part(r)
        if r > 0:
            for d in range(2):
                forward_in(r - 1, d).wait_recv()
            second_part(r - 1)
    for d in range(2):
        forward_in(CHUNKS - 1, d).wait_recv()

    def core_copy(n):
        return remote(tb.at[n], tpeer.at[n], core_send.at[n], core_recv.at[n], ctx=other)

    def piece(dest):
        return remote(cb.at[dest], r1.at[chip], one_sem.at[0], one_sem.at[1], ctx=dest * 2 + core)

    end_rows = pl.ds(3 * SPAN, SPAN)
    end_where = pl.ds(pl.multiple_of(opposite * WIDTH, WIDTH), WIDTH)
    key = acc[1, 4, :, DK:] + dot(full[opposite, end_rows, :], wv[4, end_where, DK:])
    values = []
    for order in range(4):
        values.append(value_of(3, lax.rem(2 * (1 - core) + order, 4)))
    key_t = unit_rows(key).T.astype(BF)
    kt[...] = key_t
    for order in range(4):
        n = lax.rem(2 * (1 - core) + order, 4)
        last[n] = values[order]
        total = tot[n] + dot(key_t, values[order])
        tot[n] = total
        tb[n] = total.astype(BF)
        core_copy(n).start()
        if order >= 2:
            m = order - 2
            core_copy(n).wait_recv()
            both = tot[n] + tpeer[n].astype(F32)
            cb[m * 8 : (m + 1) * 8] = both.astype(BF).reshape(8, 16, TILE)

            for dz in range(2):
                z = 2 * m + lax.rem(z_of[0] + dz, 2)
                for dx in range(4):
                    dest = 4 * z + x_of[dx]
                    if dx:
                        piece(dest).start()
                    else:
                        @pl.when(dest != chip)
                        def _():
                            piece(dest).start()

    pair_copy = remote(cb, r2.at[0], pair_sem.at[0], pair_sem.at[1], ctx=lax.rem(ctx + 2, 32))

    @pl.when(bits[0] == 0)
    def _():
        pair_copy.start()

    r1[chip] = cb[chip]
    others = pl.ds(0, CHIPS - 1)
    remote(cb.at[others], r1.at[others], one_sem.at[0], one_sem.at[1], ctx=other).wait_recv()

    piece_of = [r1[c].astype(F32) for c in range(CHIPS)]
    pair = [piece_of[4 * z] + piece_of[4 * z + 1] for z in range(4)]
    line = [pair[z] + (piece_of[4 * z + 2] + piece_of[4 * z + 3]) for z in range(4)]
    lower = line[0] + line[1]
    for c in range(CHIPS):
        z, x = c // 4, c % 4
        slot = 0
        for bit, value in ((x & 2, pair[z]), (z & 1, line[z - 1]), (z & 2, lower)):
            if bit:
                sb[3 * c + slot] = value.astype(BF)
                slot += 1

    def send_sum(dest, s):
        remote(
            sb.at[3 * dest + s - 1], r2.at[s, chip], two_send, two_recv.at[s], ctx=dest * 2 + core
        ).start()

    for dest in (2, 3):
        @pl.when(chip != dest)
        def _():
            send_sum(dest, 1)

    for s in (1, 2):
        for dx in range(4):
            dest = 4 + x_of[dx]

            @pl.when((x_count[dx] >= s - 1) & (chip != dest))
            def _():
                send_sum(dest, s)

    for s in range(1, 4):
        for dz, dx in ring:
            @pl.when((z_count[dz] + x_count[dx] >= s) & (z_of[dz] > 1))
            def _():
                send_sum(4 * z_of[dz] + x_of[dx], s)

    query = acc[1, 4, :, :DK] + dot(full[opposite, end_rows, :], wv[4, end_where, :DK])
    q[end_rows, :] = unit_rows(query).astype(BF)
    scores = score_of(3)

    def last_near(n, carry):
        near(3, n, scores, last[n])
        return carry

    lax.fori_loop(0, 4, last_near, 0)
    for n in range(2):
        core_copy(2 * (1 - core) + n).wait_recv()
    core_on = core.astype(F32)
    def core_level(r):
        rows = pl.ds(r * SPAN, SPAN)
        def body(n, carry):
            mixed[n, rows, :] = mixed[n, rows, :] + weighted(dot(q[rows, :], tpeer[n]) * core_on, n, rows, 3)
            return carry

        lax.fori_loop(0, 4, body, 0)

    core_level(0)

    def swap(s):
        return remote(r2.at[s], r2o.at[s], swap_send.at[s], swap_recv.at[s], ctx=other)

    slots = [4 * (1 - bits[0])]
    rank = 1
    for i in range(1, 4):
        slots.append(bits[i] * rank + (1 - bits[i]) * 4)
        rank = rank + bits[i]

    def far_level(r, n, m, source, i):
        rows = pl.ds(r * SPAN, SPAN)
        bucket = source[slots[i], m * 8 : m * 8 + 8].reshape(128, TILE)
        return weighted(dot(q[rows, :], bucket), n, rows, 4 + i)

    def close(r, n, x):
        rows = pl.ds(r * SPAN, SPAN)
        for h in range(2):
            one = x[:, h * DH : (h + 1) * DH]
            one = one * lax.rsqrt(jnp.mean(one * one, axis=-1, keepdims=True) + EPS)
            one = one * gain[2 * n + h]
            hid[rows, pl.ds(pl.multiple_of(n * TILE + h * DH, DH), DH)] = one.astype(BF)

    first_rows = pl.ds(0, SPAN)
    for i in range(4):
        @pl.when(bits[i] == 1)
        def _():
            if i == 0:
                pair_copy.wait_recv()
            else:
                r2[slots[i], chip] = sb[3 * chip + slots[i] - 1]
                here = r2.at[slots[i], others]
                remote(here, here, two_send, two_recv.at[slots[i]], ctx=other).wait_recv()
            swap(slots[i]).start()

        for m in range(2):
            n = 2 * core + m
            x = mixed[n, first_rows, :] + far_level(0, n, m, r2, i)
            if i < 3:
                mixed[n, first_rows, :] = x
            else:
                close(0, n, x)
    for i in range(4):
        @pl.when(bits[i] == 1)
        def _():
            swap(slots[i]).wait_recv()

        for m in range(2):
            n = 2 - 2 * core + m
            x = mixed[n, first_rows, :] + far_level(0, n, m, r2o, i)
            if i < 3:
                mixed[n, first_rows, :] = x
            else:
                close(0, n, x)

    def far(r):
        core_level(r)
        rows = pl.ds(r * SPAN, SPAN)

        def body(m, carry):
            for n, source in ((2 * core + m, r2), (2 - 2 * core + m, r2o)):
                x = mixed[n, rows, :]
                for i in range(4):
                    bucket = source[slots[i], pl.ds(pl.multiple_of(m * 8, 8), 8)].reshape(128, TILE)
                    x += weighted(dot(q[rows, :], bucket), n, rows, 4 + i)
                close(r, n, x)
            return carry

        lax.fori_loop(0, 2, body, 0)

    def opp_copy(r, d):
        return remote(popp.at[r, d], rpopp.at[r, d], opp_send.at[d, r], opp_recv.at[d, r], head=peers[d])

    def plain_copy(r, d):
        half = pl.ds(2 - 2 * d, 2)
        return remote(psum.at[r, d, half], rpsum.at[r, d, half], plain_send.at[d, r], plain_recv.at[d, r], head=peers[d])

    def sum_copy(r, d):
        half = pl.ds(2 * d, 2)
        return remote(psum.at[r, d, half], rpsum.at[r, d, half], sum_send.at[d, r], sum_recv.at[d, r], head=peers[d])

    def project(r, dest, n):
        return dot(hid[pl.ds(r * SPAN, SPAN), :], owv[dest * 4 + n])

    def opposite_part(r):
        for d in range(2):
            def body(m, carry):
                popp[r, d, m] = project(r, opposite, 2 * d + m).astype(BF)
                return carry

            lax.fori_loop(0, 2, body, 0)
            opp_copy(r, d).start()

    def neighbour_part(r):
        for d in range(2):
            def body(n, carry):
                psum[r, d, n] = project(r, peers[d], n).astype(BF)
                return carry

            lax.fori_loop(0, 4, body, 0)
            plain_copy(r, d).start()

    def relay(r):
        for d in range(2):
            opp_copy(r, d).wait_recv()
            for m in range(2):
                n = 2 * d + m
                psum[r, d, n] = (psum[r, d, n].astype(F32) + rpopp[r, d, m].astype(F32)).astype(BF)
            sum_copy(r, d).start()

    def own_part(r):
        def body(n, carry):
            pown[r, n] = project(r, me, n).astype(BF)
            return carry

        lax.fori_loop(0, 4, body, 0)

    def finish(r):
        for d in range(2):
            plain_copy(r, d).wait_recv()
            sum_copy(r, d).wait_recv()
        for n in range(4):
            total = pown[r, n].astype(F32) + rpsum[r, 0, n].astype(F32) + rpsum[r, 1, n].astype(F32)
            out[pl.ds(r * SPAN, SPAN), n * TILE : (n + 1) * TILE] = total.astype(BF)

    for r in range(CHUNKS):
        if r > 0:
            far(r)
        if r == 0:
            for load in ow_loads:
                load.wait()
        opposite_part(r)
        neighbour_part(r)
        own_part(r)
        relay(r)
        if r > 1:
            finish(r - 2)
    for r in range(CHUNKS - 2, CHUNKS):
        finish(r)

    for r in range(CHUNKS):
        for d in range(2):
            own(r, d).wait_send()
            forward(r, d).wait_send()
            opp_copy(r, d).wait_send()
            plain_copy(r, d).wait_send()
            sum_copy(r, d).wait_send()
    for n in range(4):
        core_copy(n).wait_send()
    remote(cb.at[others], r1.at[others], one_sem.at[0], one_sem.at[1], ctx=other).wait_send()

    @pl.when(bits[0] == 0)
    def _():
        pair_copy.wait_send()

    @pl.when(bits[0] == 1)
    def _():
        swap(0).wait_send()

    for j in range(4):
        @pl.when(count == j)
        def _():
            sent = sb.at[pl.ds(0, 24 - j)]
            remote(sent, sent, two_send, two_recv.at[1], ctx=other).wait_send()
            for s in range(1, j + 1):
                swap(s).wait_send()


def local(tokens, pair_weight, value_weight, output_weight, level_index, level_table, out_gain):
    any_space = pl.BlockSpec(memory_space=pl.ANY)
    vmem = pl.BlockSpec(memory_space=pltpu.VMEM)
    rows = tokens.shape[0]
    dma = pltpu.SemaphoreType.DMA
    return pl.pallas_call(
        kernel,
        out_shape=pltpu.VMEM((rows, WIDTH), BF),
        in_specs=[any_space] * 7,
        out_specs=vmem,
        scratch_shapes=[
            pltpu.VMEM((8, rows), jnp.int32),
            pltpu.VMEM((64, 16), F32),
            pltpu.VMEM((8, 1, DH), F32),
            pltpu.VMEM((4, rows, WIDTH), BF),
            pltpu.VMEM((5, 4 * WIDTH, TILE), BF),
            pltpu.VMEM((16, WIDTH, TILE), BF),
            pltpu.VMEM((2, 5, SPAN, TILE), F32),
            pltpu.VMEM((4, rows, 128), F32),
            pltpu.VMEM((rows, DK), BF),
            pltpu.VMEM((DK, SPAN), BF),
            pltpu.VMEM((4, SPAN, TILE), BF),
            pltpu.VMEM((4, DK, TILE), F32),
            pltpu.VMEM((4, DK, TILE), BF),
            pltpu.VMEM((4, DK, TILE), BF),
            pltpu.VMEM((4, DK, TILE), F32),
            pltpu.VMEM((4, DK, TILE), BF),
            pltpu.VMEM((4, DK, TILE), BF),
            pltpu.VMEM((4, rows, TILE), F32),
            pltpu.VMEM((CHIPS, 16, TILE), BF),
            pltpu.VMEM((CHIPS, 16, TILE), BF),
            pltpu.VMEM((3 * CHIPS, 16, TILE), BF),
            pltpu.VMEM((5, CHIPS, 16, TILE), BF),
            pltpu.VMEM((5, CHIPS, 16, TILE), BF),
            pltpu.VMEM((rows, WIDTH), BF),
            pltpu.VMEM((CHUNKS, 2, 2, SPAN, TILE), BF),
            pltpu.VMEM((CHUNKS, 2, 2, SPAN, TILE), BF),
            pltpu.VMEM((CHUNKS, 2, 4, SPAN, TILE), BF),
            pltpu.VMEM((CHUNKS, 2, 4, SPAN, TILE), BF),
            pltpu.VMEM((CHUNKS, 4, SPAN, TILE), BF),
            dma((25,)),
            dma((2, CHUNKS)),
            dma((2, CHUNKS)),
            dma((2, CHUNKS)),
            dma((2, CHUNKS)),
            dma((4,)),
            dma((4,)),
            dma((2,)),
            dma((2,)),
            dma(()),
            dma((4,)),
            dma((4,)),
            dma((4,)),
            dma((2, CHUNKS)),
            dma((2, CHUNKS)),
            dma((2, CHUNKS)),
            dma((2, CHUNKS)),
            dma((2, CHUNKS)),
            dma((2, CHUNKS)),
        ],
        compiler_params=pltpu.CompilerParams(
            collective_id=0, has_side_effects=True, vmem_limit_bytes=56 * 1024 * 1024
        ),
        name="layer",
    )(
        tokens, pair_weight, value_weight, output_weight, level_index.T,
        level_table.transpose(0, 2, 1).reshape(64, 16), out_gain.reshape(8, 1, 128),
    )


def solution(mesh):
    return jax.shard_map(
        local,
        mesh=mesh,
        in_specs=(
            P("ctx", "head"),
            P(),
            P(None, "head"),
            P("head", None),
            P("ctx", None),
            P(None, None, "head"),
            P("head"),
        ),
        out_specs=P("ctx", "head"),
        check_vma=False,
    )
```

```python
import math

import jax
import jax.numpy as jnp
from jax import lax
from jax.experimental import pallas as pl
from jax.experimental.pallas import tpu as pltpu
from jax.sharding import PartitionSpec as P

DH = 128
DK = 128
SPAN = 128
EPS = 1e-06
CHUNKS = 4
WIDTH = 1024
TILE = 256
CHIPS = 16
MESH = pl.DeviceIdType.MESH
BF = jnp.bfloat16
F32 = jnp.float32


def dot(a, b):
    return jnp.dot(a, b, preferred_element_type=F32)


def unit_rows(values):
    scale = lax.rsqrt(jnp.mean(values * values, axis=-1, keepdims=True) + EPS)
    return values * scale / math.sqrt(values.shape[-1])


def kernel(
    tok, pw, vw, ow, lidx_in, ltab_in, gain_in, out,
    lidx, ltab, gain,
    full, wv, owv, acc, mixn, q, kt, last, s01, s0b, s2b, tot, tb, tpeer, mixed,
    cb, r1, sb, r2, r2o, hid, popp, rpopp, psum, rpsum, pown,
    w_sem, own_send, own_recv, fwd_send, fwd_recv, core_send, core_recv, one_sem, pair_sem, two_send, two_recv,
    swap_send, swap_recv,
    opp_send, opp_recv, plain_send, plain_recv, sum_send, sum_recv,
):
    me = lax.axis_index("head")
    ctx = lax.axis_index("ctx")
    right = lax.rem(me + 1, 4)
    left = lax.rem(me + 3, 4)
    opposite = lax.rem(me + 2, 4)
    core = lax.rem(ctx, 2)
    chip = lax.div(ctx, 2)
    other = ctx + 1 - 2 * core
    bits = [lax.rem(lax.div(chip, 1 << i), 2) for i in range(4)]
    count = bits[1] + bits[2] + bits[3]
    z_of = [lax.rem(lax.div(chip, 4) + d, 4) for d in range(4)]
    x_of = [lax.rem(lax.rem(chip, 4) + d, 4) for d in range(4)]
    z_count = [lax.rem(z, 2) + lax.div(z, 2) for z in z_of]
    x_count = [lax.div(x, 2) for x in x_of]
    ring = [(dz, dx) for dz in range(4) for dx in range(4) if dz or dx]

    def remote(src, dst, send, recv, **axes):
        return pltpu.make_async_remote_copy(
            src_ref=src, dst_ref=dst, send_sem=send, recv_sem=recv,
            device_id=axes, device_id_type=MESH,
        )

    loads = [
        pltpu.make_async_copy(pw, wv.at[4], w_sem.at[4]),
    ]
    for n in range(4):
        loads.append(pltpu.make_async_copy(vw.at[:, pl.ds(n * TILE, TILE)], wv.at[n], w_sem.at[n]))
    tok_load = pltpu.make_async_copy(tok, full.at[me], w_sem.at[5])
    ow_loads = [
        pltpu.make_async_copy(ow.at[:, pl.ds(t * TILE, TILE)], owv.at[t], w_sem.at[6 + t])
        for t in range(16)
    ]

    barrier = pltpu.get_barrier_semaphore()
    for peer in (left, right):
        pl.semaphore_signal(barrier, inc=1, device_id={"head": peer}, device_id_type=MESH)
    pl.semaphore_signal(barrier, inc=1, device_id={"ctx": other}, device_id_type=MESH)

    for dz, dx in ring:
        dest = (4 * z_of[dz] + x_of[dx]) * 2 + core
        pl.semaphore_signal(barrier, inc=1, device_id={"ctx": dest}, device_id_type=MESH)
    small = [
        pltpu.make_async_copy(src, dst, w_sem.at[22 + i])
        for i, (src, dst) in enumerate(((lidx_in, lidx), (ltab_in, ltab), (gain_in, gain)))
    ]
    for load in small:
        load.start()
    tok_load.start()
    for load in loads:
        load.start()
    pl.semaphore_wait(barrier, 3 + CHIPS - 1)

    peers = (right, left)
    HALF = SPAN // 2

    def own(r, d):
        rows = pl.ds(r * SPAN, SPAN)
        return remote(tok.at[rows], full.at[me, rows], own_send.at[d, r], own_recv.at[d, r], head=peers[d])

    def own_in(r, d):
        rows = pl.ds(r * SPAN, SPAN)
        slot = (left, right)[d]
        return remote(tok.at[rows], full.at[slot, rows], own_send.at[d, r], own_recv.at[d, r], head=peers[d])

    def forward(r, d):
        rows = pl.ds(r * SPAN + d * HALF, HALF)
        slot = (left, right)[d]
        return remote(full.at[slot, rows], full.at[slot, rows], fwd_send.at[d, r], fwd_recv.at[d, r], head=peers[d])

    def forward_in(r, d):
        rows = pl.ds(r * SPAN + d * HALF, HALF)
        return remote(full.at[opposite, rows], full.at[opposite, rows], fwd_send.at[d, r], fwd_recv.at[d, r], head=peers[d])

    for r in range(2):
        for d in range(2):
            own(r, d).start()

    for load in small:
        load.wait()
    row = lax.broadcasted_iota(jnp.int32, (128, 8), 0)
    spread = jnp.where(row // 16 == lax.broadcasted_iota(jnp.int32, (128, 8), 1), 1.0, 0.0).astype(BF)
    wanted = dot(spread, lidx[...].astype(F32).astype(BF))
    entry = lax.broadcasted_iota(jnp.int32, (128, CHUNKS * SPAN), 0) % 16
    onehot = jnp.where(wanted == entry.astype(F32), 1.0, 0.0).T
    exact = lax.Precision.HIGHEST
    level_of = lax.broadcasted_iota(jnp.int32, (64, 128), 0) // 8
    lane_level = lax.broadcasted_iota(jnp.int32, (64, 128), 1) // 16
    placed = jnp.where(level_of == lane_level, jnp.concatenate([ltab[...]] * 8, axis=1), 0.0)
    column = lax.broadcasted_iota(jnp.int32, (128, 64), 0)
    source = lax.broadcasted_iota(jnp.int32, (128, 64), 1)
    for n in range(4):
        take = jnp.where((column < 16) & (source == (column // 2) * 8 + 2 * n + column % 2), 1.0, 0.0)
        table = jnp.dot(take, placed, preferred_element_type=F32, precision=exact).T
        mixn[n] = jnp.dot(onehot, table, preferred_element_type=F32, precision=exact)
    r2[4] = jnp.zeros((CHIPS, 16, TILE), BF)
    r2o[4] = jnp.zeros((CHIPS, 16, TILE), BF)

    def weighted(value, n, rows, level):
        parts = []
        for h in range(2):
            w = mixn[n, rows, 2 * level + h : 2 * level + h + 1]
            parts.append(value[:, h * DH : (h + 1) * DH] * w)
        return jnp.concatenate(parts, axis=1)

    for load in loads:
        load.wait()
    tok_load.wait()
    for load in ow_loads:
        load.start()

    def first_part(r):
        rows = pl.ds(r * SPAN, SPAN)

        def body(n, carry):
            total = None
            for slot in (me, left, right):
                term = dot(full[slot, rows, :], wv[n, pl.ds(pl.multiple_of(slot * WIDTH, WIDTH), WIDTH), :])
                total = term if total is None else total + term
            acc[r % 2, n] = total
            return carry

        lax.fori_loop(0, 5, body, 0)

    def heads_of(r):
        where = pl.ds(pl.multiple_of(opposite * WIDTH, WIDTH), WIDTH)
        rows = pl.ds(r * SPAN, SPAN)
        paired = acc[r % 2, 4] + dot(full[opposite, rows, :], wv[4, where, :])
        q[rows, :] = unit_rows(paired[:, :DK]).astype(BF)
        kt[...] = unit_rows(paired[:, DK:]).T.astype(BF)

    def value_of(r, n):
        where = pl.ds(pl.multiple_of(opposite * WIDTH, WIDTH), WIDTH)
        rows = pl.ds(r * SPAN, SPAN)
        return (acc[r % 2, n] + dot(full[opposite, rows, :], wv[n, where, :])).astype(BF)

    def score_of(r):
        scores = dot(q[pl.ds(r * SPAN, SPAN), :], kt[...])
        t = lax.broadcasted_iota(jnp.int32, (SPAN, SPAN), 0)
        s = lax.broadcasted_iota(jnp.int32, (SPAN, SPAN), 1)
        return jnp.where(t >= s, scores, 0.0).astype(BF)

    def near(r, n, scores, value):
        rows = pl.ds(r * SPAN, SPAN)
        query = q[rows, :]
        result = weighted(dot(scores, value), n, rows, 0)
        if r == 1:
            result += weighted(dot(query, s0b[n]), n, rows, 1)
        if r == 3:
            result += weighted(dot(query, s2b[n]), n, rows, 1)
        if r >= 2:
            result += weighted(dot(query, s01[n].astype(BF)), n, rows, 2)
        mixed[n, rows, :] = result

    def second_part(r):
        heads_of(r)
        scores = score_of(r)

        def body(n, carry):
            value = value_of(r, n)
            near(r, n, scores, value)
            state = dot(kt[...], value)
            if r == 0:
                s01[n] = state
                s0b[n] = state.astype(BF)
            elif r == 1:
                s01[n] = s01[n] + state
            else:
                s2b[n] = state.astype(BF)
                tot[n] = s01[n] + state
            return carry

        lax.fori_loop(0, 4, body, 0)

    for r in range(CHUNKS):
        for d in range(2):
            own_in(r, d).wait_recv()
            forward(r, d).start()
        if r + 2 < CHUNKS:
            for d in range(2):
                own(r + 2, d).start()
        first_part(r)
        if r > 0:
            for d in range(2):
                forward_in(r - 1, d).wait_recv()
            second_part(r - 1)
    for d in range(2):
        forward_in(CHUNKS - 1, d).wait_recv()

    def core_copy(n):
        return remote(tb.at[n], tpeer.at[n], core_send.at[n], core_recv.at[n], ctx=other)

    def piece(dest):
        return remote(cb.at[dest], r1.at[chip], one_sem.at[0], one_sem.at[1], ctx=dest * 2 + core)

    end_rows = pl.ds(3 * SPAN, SPAN)
    end_where = pl.ds(pl.multiple_of(opposite * WIDTH, WIDTH), WIDTH)
    key = acc[1, 4, :, DK:] + dot(full[opposite, end_rows, :], wv[4, end_where, DK:])
    values = []
    for order in range(4):
        values.append(value_of(3, lax.rem(2 * (1 - core) + order, 4)))
    key_t = unit_rows(key).T.astype(BF)
    kt[...] = key_t
    for order in range(4):
        n = lax.rem(2 * (1 - core) + order, 4)
        last[n] = values[order]
        total = tot[n] + dot(key_t, values[order])
        tot[n] = total
        tb[n] = total.astype(BF)
        core_copy(n).start()
        if order >= 2:
            m = order - 2
            core_copy(n).wait_recv()
            both = tot[n] + tpeer[n].astype(F32)
            cb[m * 8 : (m + 1) * 8] = both.astype(BF).reshape(8, 16, TILE)

            for dz in range(2):
                z = 2 * m + lax.rem(z_of[0] + dz, 2)
                for dx in range(4):
                    dest = 4 * z + x_of[dx]
                    if dx:
                        piece(dest).start()
                    else:
                        @pl.when(dest != chip)
                        def _():
                            piece(dest).start()

    pair_copy = remote(cb, r2.at[0], pair_sem.at[0], pair_sem.at[1], ctx=lax.rem(ctx + 2, 32))

    @pl.when(bits[0] == 0)
    def _():
        pair_copy.start()

    r1[chip] = cb[chip]
    others = pl.ds(0, CHIPS - 1)
    remote(cb.at[others], r1.at[others], one_sem.at[0], one_sem.at[1], ctx=other).wait_recv()

    piece_of = [r1[c].astype(F32) for c in range(CHIPS)]
    pair = [piece_of[4 * z] + piece_of[4 * z + 1] for z in range(4)]
    line = [pair[z] + (piece_of[4 * z + 2] + piece_of[4 * z + 3]) for z in range(4)]
    lower = line[0] + line[1]
    for c in range(CHIPS):
        z, x = c // 4, c % 4
        slot = 0
        for bit, value in ((x & 2, pair[z]), (z & 1, line[z - 1]), (z & 2, lower)):
            if bit:
                sb[3 * c + slot] = value.astype(BF)
                slot += 1

    def send_sum(dest, s):
        remote(
            sb.at[3 * dest + s - 1], r2.at[s, chip], two_send, two_recv.at[s], ctx=dest * 2 + core
        ).start()

    for dest in (2, 3):
        @pl.when(chip != dest)
        def _():
            send_sum(dest, 1)

    for s in (1, 2):
        for dx in range(4):
            dest = 4 + x_of[dx]

            @pl.when((x_count[dx] >= s - 1) & (chip != dest))
            def _():
                send_sum(dest, s)

    for s in range(1, 4):
        for dz, dx in ring:
            @pl.when((z_count[dz] + x_count[dx] >= s) & (z_of[dz] > 1))
            def _():
                send_sum(4 * z_of[dz] + x_of[dx], s)

    query = acc[1, 4, :, :DK] + dot(full[opposite, end_rows, :], wv[4, end_where, :DK])
    q[end_rows, :] = unit_rows(query).astype(BF)
    scores = score_of(3)

    def last_near(n, carry):
        near(3, n, scores, last[n])
        return carry

    lax.fori_loop(0, 4, last_near, 0)
    for n in range(2):
        core_copy(2 * (1 - core) + n).wait_recv()
    core_on = core.astype(F32)
    def core_level(r):
        rows = pl.ds(r * SPAN, SPAN)
        def body(n, carry):
            mixed[n, rows, :] = mixed[n, rows, :] + weighted(dot(q[rows, :], tpeer[n]) * core_on, n, rows, 3)
            return carry

        lax.fori_loop(0, 4, body, 0)

    core_level(0)

    def swap(s):
        return remote(r2.at[s], r2o.at[s], swap_send.at[s], swap_recv.at[s], ctx=other)

    slots = [4 * (1 - bits[0])]
    rank = 1
    for i in range(1, 4):
        slots.append(bits[i] * rank + (1 - bits[i]) * 4)
        rank = rank + bits[i]

    def far_level(r, n, m, source, i):
        rows = pl.ds(r * SPAN, SPAN)
        bucket = source[slots[i], m * 8 : m * 8 + 8].reshape(128, TILE)
        return weighted(dot(q[rows, :], bucket), n, rows, 4 + i)

    def close(r, n, x):
        rows = pl.ds(r * SPAN, SPAN)
        for h in range(2):
            one = x[:, h * DH : (h + 1) * DH]
            one = one * lax.rsqrt(jnp.mean(one * one, axis=-1, keepdims=True) + EPS)
            one = one * gain[2 * n + h]
            hid[rows, pl.ds(pl.multiple_of(n * TILE + h * DH, DH), DH)] = one.astype(BF)

    first_rows = pl.ds(0, SPAN)
    for i in range(4):
        @pl.when(bits[i] == 1)
        def _():
            if i == 0:
                pair_copy.wait_recv()
            else:
                r2[slots[i], chip] = sb[3 * chip + slots[i] - 1]
                here = r2.at[slots[i], others]
                remote(here, here, two_send, two_recv.at[slots[i]], ctx=other).wait_recv()
            swap(slots[i]).start()

        for m in range(2):
            n = 2 * core + m
            x = mixed[n, first_rows, :] + far_level(0, n, m, r2, i)
            if i < 3:
                mixed[n, first_rows, :] = x
            else:
                close(0, n, x)
    for i in range(4):
        @pl.when(bits[i] == 1)
        def _():
            swap(slots[i]).wait_recv()

        for m in range(2):
            n = 2 - 2 * core + m
            x = mixed[n, first_rows, :] + far_level(0, n, m, r2o, i)
            if i < 3:
                mixed[n, first_rows, :] = x
            else:
                close(0, n, x)

    def far(r):
        core_level(r)
        rows = pl.ds(r * SPAN, SPAN)

        def body(m, carry):
            for n, source in ((2 * core + m, r2), (2 - 2 * core + m, r2o)):
                x = mixed[n, rows, :]
                for i in range(4):
                    bucket = source[slots[i], pl.ds(pl.multiple_of(m * 8, 8), 8)].reshape(128, TILE)
                    x += weighted(dot(q[rows, :], bucket), n, rows, 4 + i)
                close(r, n, x)
            return carry

        lax.fori_loop(0, 2, body, 0)

    def opp_copy(r, d):
        return remote(popp.at[r, d], rpopp.at[r, d], opp_send.at[d, r], opp_recv.at[d, r], head=peers[d])

    def plain_copy(r, d):
        half = pl.ds(2 - 2 * d, 2)
        return remote(psum.at[r, d, half], rpsum.at[r, d, half], plain_send.at[d, r], plain_recv.at[d, r], head=peers[d])

    def sum_copy(r, d):
        half = pl.ds(2 * d, 2)
        return remote(psum.at[r, d, half], rpsum.at[r, d, half], sum_send.at[d, r], sum_recv.at[d, r], head=peers[d])

    def project(r, dest, n):
        return dot(hid[pl.ds(r * SPAN, SPAN), :], owv[dest * 4 + n])

    def opposite_part(r):
        for m in range(2):
            for d in range(2):
                popp[r, d, m] = project(r, opposite, 2 * d + m).astype(BF)
                remote(
                    popp.at[r, d, m], rpopp.at[r, d, m], opp_send.at[d, r], opp_recv.at[d, r], head=peers[d]
                ).start()

    def neighbour_part(r):
        for d in range(2):
            def body(n, carry):
                psum[r, d, n] = project(r, peers[d], n).astype(BF)
                return carry

            lax.fori_loop(0, 4, body, 0)
            plain_copy(r, d).start()

    def relay(r):
        for d in range(2):
            opp_copy(r, d).wait_recv()
            for m in range(2):
                n = 2 * d + m
                psum[r, d, n] = (psum[r, d, n].astype(F32) + rpopp[r, d, m].astype(F32)).astype(BF)
            sum_copy(r, d).start()

    def own_part(r):
        def body(n, carry):
            pown[r, n] = project(r, me, n).astype(BF)
            return carry

        lax.fori_loop(0, 4, body, 0)

    def finish(r):
        for d in range(2):
            plain_copy(r, d).wait_recv()
            sum_copy(r, d).wait_recv()
        for n in range(4):
            total = pown[r, n].astype(F32) + rpsum[r, 0, n].astype(F32) + rpsum[r, 1, n].astype(F32)
            out[pl.ds(r * SPAN, SPAN), n * TILE : (n + 1) * TILE] = total.astype(BF)

    for load in ow_loads:
        load.wait()
    for r in range(CHUNKS):
        opposite_part(r)
        neighbour_part(r)
        own_part(r)
        if r + 1 < CHUNKS:
            far(r + 1)
        relay(r)
        if r > 1:
            finish(r - 2)
    for r in range(CHUNKS - 2, CHUNKS):
        finish(r)

    for r in range(CHUNKS):
        for d in range(2):
            own(r, d).wait_send()
            forward(r, d).wait_send()
            opp_copy(r, d).wait_send()
            plain_copy(r, d).wait_send()
            sum_copy(r, d).wait_send()
    for n in range(4):
        core_copy(n).wait_send()
    remote(cb.at[others], r1.at[others], one_sem.at[0], one_sem.at[1], ctx=other).wait_send()

    @pl.when(bits[0] == 0)
    def _():
        pair_copy.wait_send()

    @pl.when(bits[0] == 1)
    def _():
        swap(0).wait_send()

    for j in range(4):
        @pl.when(count == j)
        def _():
            sent = sb.at[pl.ds(0, 24 - j)]
            remote(sent, sent, two_send, two_recv.at[1], ctx=other).wait_send()
            for s in range(1, j + 1):
                swap(s).wait_send()


def local(tokens, pair_weight, value_weight, output_weight, level_index, level_table, out_gain):
    any_space = pl.BlockSpec(memory_space=pl.ANY)
    vmem = pl.BlockSpec(memory_space=pltpu.VMEM)
    rows = tokens.shape[0]
    dma = pltpu.SemaphoreType.DMA
    return pl.pallas_call(
        kernel,
        out_shape=pltpu.VMEM((rows, WIDTH), BF),
        in_specs=[any_space] * 7,
        out_specs=vmem,
        scratch_shapes=[
            pltpu.VMEM((8, rows), jnp.int32),
            pltpu.VMEM((64, 16), F32),
            pltpu.VMEM((8, 1, DH), F32),
            pltpu.VMEM((4, rows, WIDTH), BF),
            pltpu.VMEM((5, 4 * WIDTH, TILE), BF),
            pltpu.VMEM((16, WIDTH, TILE), BF),
            pltpu.VMEM((2, 5, SPAN, TILE), F32),
            pltpu.VMEM((4, rows, 128), F32),
            pltpu.VMEM((rows, DK), BF),
            pltpu.VMEM((DK, SPAN), BF),
            pltpu.VMEM((4, SPAN, TILE), BF),
            pltpu.VMEM((4, DK, TILE), F32),
            pltpu.VMEM((4, DK, TILE), BF),
            pltpu.VMEM((4, DK, TILE), BF),
            pltpu.VMEM((4, DK, TILE), F32),
            pltpu.VMEM((4, DK, TILE), BF),
            pltpu.VMEM((4, DK, TILE), BF),
            pltpu.VMEM((4, rows, TILE), F32),
            pltpu.VMEM((CHIPS, 16, TILE), BF),
            pltpu.VMEM((CHIPS, 16, TILE), BF),
            pltpu.VMEM((3 * CHIPS, 16, TILE), BF),
            pltpu.VMEM((5, CHIPS, 16, TILE), BF),
            pltpu.VMEM((5, CHIPS, 16, TILE), BF),
            pltpu.VMEM((rows, WIDTH), BF),
            pltpu.VMEM((CHUNKS, 2, 2, SPAN, TILE), BF),
            pltpu.VMEM((CHUNKS, 2, 2, SPAN, TILE), BF),
            pltpu.VMEM((CHUNKS, 2, 4, SPAN, TILE), BF),
            pltpu.VMEM((CHUNKS, 2, 4, SPAN, TILE), BF),
            pltpu.VMEM((CHUNKS, 4, SPAN, TILE), BF),
            dma((25,)),
            dma((2, CHUNKS)),
            dma((2, CHUNKS)),
            dma((2, CHUNKS)),
            dma((2, CHUNKS)),
            dma((4,)),
            dma((4,)),
            dma((2,)),
            dma((2,)),
            dma(()),
            dma((4,)),
            dma((4,)),
            dma((4,)),
            dma((2, CHUNKS)),
            dma((2, CHUNKS)),
            dma((2, CHUNKS)),
            dma((2, CHUNKS)),
            dma((2, CHUNKS)),
            dma((2, CHUNKS)),
        ],
        compiler_params=pltpu.CompilerParams(
            collective_id=0, has_side_effects=True, vmem_limit_bytes=56 * 1024 * 1024
        ),
        name="layer",
    )(
        tokens, pair_weight, value_weight, output_weight, level_index.T,
        level_table.transpose(0, 2, 1).reshape(64, 16), out_gain.reshape(8, 1, 128),
    )


def solution(mesh):
    return jax.shard_map(
        local,
        mesh=mesh,
        in_specs=(
            P("ctx", "head"),
            P(),
            P(None, "head"),
            P("head", None),
            P("ctx", None),
            P(None, None, "head"),
            P("head"),
        ),
        out_specs=P("ctx", "head"),
        check_vma=False,
    )
```

```python
import math

import jax
import jax.numpy as jnp
from jax import lax
from jax.experimental import pallas as pl
from jax.experimental.pallas import tpu as pltpu
from jax.sharding import PartitionSpec as P

DH = 128
DK = 128
SPAN = 128
EPS = 1e-06
CHUNKS = 4
WIDTH = 1024
TILE = 256
CHIPS = 16
MESH = pl.DeviceIdType.MESH
BF = jnp.bfloat16
F32 = jnp.float32


def dot(a, b):
    return jnp.dot(a, b, preferred_element_type=F32)


def unit_rows(values):
    scale = lax.rsqrt(jnp.mean(values * values, axis=-1, keepdims=True) + EPS)
    return values * scale / math.sqrt(values.shape[-1])


def kernel(
    tok, pw, vw, ow, lidx_in, ltab_in, gain_in, out,
    lidx, ltab, gain,
    full, wv, owv, acc, mixn, q, kt, last, s01, s0b, s2b, tot, tb, tpeer, mixed,
    cb, r1, sb, r2, r2o, hid, popp, rpopp, psum, rpsum, pown,
    w_sem, own_send, own_recv, fwd_send, fwd_recv, core_send, core_recv, one_sem, pair_sem, two_send, two_recv,
    swap_send, swap_recv,
    opp_send, opp_recv, plain_send, plain_recv, sum_send, sum_recv,
):
    me = lax.axis_index("head")
    ctx = lax.axis_index("ctx")
    right = lax.rem(me + 1, 4)
    left = lax.rem(me + 3, 4)
    opposite = lax.rem(me + 2, 4)
    core = lax.rem(ctx, 2)
    chip = lax.div(ctx, 2)
    other = ctx + 1 - 2 * core
    bits = [lax.rem(lax.div(chip, 1 << i), 2) for i in range(4)]
    count = bits[1] + bits[2] + bits[3]
    z_of = [lax.rem(lax.div(chip, 4) + d, 4) for d in range(4)]
    x_of = [lax.rem(lax.rem(chip, 4) + d, 4) for d in range(4)]
    z_count = [lax.rem(z, 2) + lax.div(z, 2) for z in z_of]
    x_count = [lax.div(x, 2) for x in x_of]
    ring = [(dz, dx) for dz in range(4) for dx in range(4) if dz or dx]

    def remote(src, dst, send, recv, **axes):
        return pltpu.make_async_remote_copy(
            src_ref=src, dst_ref=dst, send_sem=send, recv_sem=recv,
            device_id=axes, device_id_type=MESH,
        )

    loads = [
        pltpu.make_async_copy(pw, wv.at[4], w_sem.at[4]),
    ]
    for n in range(4):
        loads.append(pltpu.make_async_copy(vw.at[:, pl.ds(n * TILE, TILE)], wv.at[n], w_sem.at[n]))
    tok_load = pltpu.make_async_copy(tok, full.at[me], w_sem.at[5])
    ow_loads = [
        pltpu.make_async_copy(ow.at[:, pl.ds(t * TILE, TILE)], owv.at[t], w_sem.at[6 + t])
        for t in range(16)
    ]

    barrier = pltpu.get_barrier_semaphore()
    for peer in (left, right):
        pl.semaphore_signal(barrier, inc=1, device_id={"head": peer}, device_id_type=MESH)
    pl.semaphore_signal(barrier, inc=1, device_id={"ctx": other}, device_id_type=MESH)

    for dz, dx in sorted(ring, key=lambda step: (2, 1, 3, 0).index(step[0])):
        dest = (4 * z_of[dz] + x_of[dx]) * 2 + core
        pl.semaphore_signal(barrier, inc=1, device_id={"ctx": dest}, device_id_type=MESH)
    small = [
        pltpu.make_async_copy(src, dst, w_sem.at[22 + i])
        for i, (src, dst) in enumerate(((lidx_in, lidx), (ltab_in, ltab), (gain_in, gain)))
    ]
    for load in small:
        load.start()
    tok_load.start()
    for load in loads:
        load.start()
    pl.semaphore_wait(barrier, 3 + CHIPS - 1)

    peers = (right, left)
    HALF = SPAN // 2

    def own(r, d):
        rows = pl.ds(r * SPAN, SPAN)
        return remote(tok.at[rows], full.at[me, rows], own_send.at[d, r], own_recv.at[d, r], head=peers[d])

    def own_in(r, d):
        rows = pl.ds(r * SPAN, SPAN)
        slot = (left, right)[d]
        return remote(tok.at[rows], full.at[slot, rows], own_send.at[d, r], own_recv.at[d, r], head=peers[d])

    def forward(r, d):
        rows = pl.ds(r * SPAN + d * HALF, HALF)
        slot = (left, right)[d]
        return remote(full.at[slot, rows], full.at[slot, rows], fwd_send.at[d, r], fwd_recv.at[d, r], head=peers[d])

    def forward_in(r, d):
        rows = pl.ds(r * SPAN + d * HALF, HALF)
        return remote(full.at[opposite, rows], full.at[opposite, rows], fwd_send.at[d, r], fwd_recv.at[d, r], head=peers[d])

    for r in range(2):
        for d in range(2):
            own(r, d).start()

    for load in small:
        load.wait()
    row = lax.broadcasted_iota(jnp.int32, (128, 8), 0)
    spread = jnp.where(row // 16 == lax.broadcasted_iota(jnp.int32, (128, 8), 1), 1.0, 0.0).astype(BF)
    wanted = dot(spread, lidx[...].astype(F32).astype(BF))
    entry = lax.broadcasted_iota(jnp.int32, (128, CHUNKS * SPAN), 0) % 16
    onehot = jnp.where(wanted == entry.astype(F32), 1.0, 0.0).T
    exact = lax.Precision.HIGHEST
    level_of = lax.broadcasted_iota(jnp.int32, (64, 128), 0) // 8
    lane_level = lax.broadcasted_iota(jnp.int32, (64, 128), 1) // 16
    placed = jnp.where(level_of == lane_level, jnp.concatenate([ltab[...]] * 8, axis=1), 0.0)
    column = lax.broadcasted_iota(jnp.int32, (128, 64), 0)
    source = lax.broadcasted_iota(jnp.int32, (128, 64), 1)
    for n in range(4):
        take = jnp.where((column < 16) & (source == (column // 2) * 8 + 2 * n + column % 2), 1.0, 0.0)
        table = jnp.dot(take, placed, preferred_element_type=F32, precision=exact).T
        mixn[n] = jnp.dot(onehot, table, preferred_element_type=F32, precision=exact)
    r2[4] = jnp.zeros((CHIPS, 16, TILE), BF)
    r2o[4] = jnp.zeros((CHIPS, 16, TILE), BF)

    def weighted(value, n, rows, level):
        parts = []
        for h in range(2):
            w = mixn[n, rows, 2 * level + h : 2 * level + h + 1]
            parts.append(value[:, h * DH : (h + 1) * DH] * w)
        return jnp.concatenate(parts, axis=1)

    for load in loads:
        load.wait()
    tok_load.wait()
    for load in ow_loads:
        load.start()

    def first_part(r):
        rows = pl.ds(r * SPAN, SPAN)

        def body(n, carry):
            total = None
            for slot in (me, left, right):
                term = dot(full[slot, rows, :], wv[n, pl.ds(pl.multiple_of(slot * WIDTH, WIDTH), WIDTH), :])
                total = term if total is None else total + term
            acc[r % 2, n] = total
            return carry

        lax.fori_loop(0, 5, body, 0)

    def heads_of(r):
        where = pl.ds(pl.multiple_of(opposite * WIDTH, WIDTH), WIDTH)
        rows = pl.ds(r * SPAN, SPAN)
        paired = acc[r % 2, 4] + dot(full[opposite, rows, :], wv[4, where, :])
        q[rows, :] = unit_rows(paired[:, :DK]).astype(BF)
        kt[...] = unit_rows(paired[:, DK:]).T.astype(BF)

    def value_of(r, n):
        where = pl.ds(pl.multiple_of(opposite * WIDTH, WIDTH), WIDTH)
        rows = pl.ds(r * SPAN, SPAN)
        return (acc[r % 2, n] + dot(full[opposite, rows, :], wv[n, where, :])).astype(BF)

    def score_of(r):
        scores = dot(q[pl.ds(r * SPAN, SPAN), :], kt[...])
        t = lax.broadcasted_iota(jnp.int32, (SPAN, SPAN), 0)
        s = lax.broadcasted_iota(jnp.int32, (SPAN, SPAN), 1)
        return jnp.where(t >= s, scores, 0.0).astype(BF)

    def near(r, n, scores, value):
        rows = pl.ds(r * SPAN, SPAN)
        query = q[rows, :]
        result = weighted(dot(scores, value), n, rows, 0)
        if r == 1:
            result += weighted(dot(query, s0b[n]), n, rows, 1)
        if r == 3:
            result += weighted(dot(query, s2b[n]), n, rows, 1)
        if r >= 2:
            result += weighted(dot(query, s01[n].astype(BF)), n, rows, 2)
        mixed[n, rows, :] = result

    def second_part(r):
        heads_of(r)
        scores = score_of(r)

        def body(n, carry):
            value = value_of(r, n)
            near(r, n, scores, value)
            state = dot(kt[...], value)
            if r == 0:
                s01[n] = state
                s0b[n] = state.astype(BF)
            elif r == 1:
                s01[n] = s01[n] + state
            else:
                s2b[n] = state.astype(BF)
                tot[n] = s01[n] + state
            return carry

        lax.fori_loop(0, 4, body, 0)

    for r in range(CHUNKS):
        for d in range(2):
            own_in(r, d).wait_recv()
            forward(r, d).start()
        if r + 2 < CHUNKS:
            for d in range(2):
                own(r + 2, d).start()
        first_part(r)
        if r > 0:
            for d in range(2):
                forward_in(r - 1, d).wait_recv()
            second_part(r - 1)
    for d in range(2):
        forward_in(CHUNKS - 1, d).wait_recv()

    def core_copy(n):
        return remote(tb.at[n], tpeer.at[n], core_send.at[n], core_recv.at[n], ctx=other)

    def piece(dest):
        return remote(cb.at[dest], r1.at[chip], one_sem.at[0], one_sem.at[1], ctx=dest * 2 + core)

    end_rows = pl.ds(3 * SPAN, SPAN)
    end_where = pl.ds(pl.multiple_of(opposite * WIDTH, WIDTH), WIDTH)
    key = acc[1, 4, :, DK:] + dot(full[opposite, end_rows, :], wv[4, end_where, DK:])
    values = []
    for order in range(4):
        values.append(value_of(3, lax.rem(2 * (1 - core) + order, 4)))
    key_t = unit_rows(key).T.astype(BF)
    kt[...] = key_t
    for order in range(4):
        n = lax.rem(2 * (1 - core) + order, 4)
        last[n] = values[order]
        total = tot[n] + dot(key_t, values[order])
        tot[n] = total
        tb[n] = total.astype(BF)
        core_copy(n).start()
        if order >= 2:
            m = order - 2
            core_copy(n).wait_recv()
            both = tot[n] + tpeer[n].astype(F32)
            cb[m * 8 : (m + 1) * 8] = both.astype(BF).reshape(8, 16, TILE)

            for dz in range(2):
                z = 2 * m + lax.rem(z_of[0] + dz, 2)
                for dx in range(4):
                    dest = 4 * z + x_of[dx]
                    if dx:
                        piece(dest).start()
                    else:
                        @pl.when(dest != chip)
                        def _():
                            piece(dest).start()

    pair_copy = remote(cb, r2.at[0], pair_sem.at[0], pair_sem.at[1], ctx=lax.rem(ctx + 2, 32))

    @pl.when(bits[0] == 0)
    def _():
        pair_copy.start()

    r1[chip] = cb[chip]
    others = pl.ds(0, CHIPS - 1)
    remote(cb.at[others], r1.at[others], one_sem.at[0], one_sem.at[1], ctx=other).wait_recv()

    piece_of = [r1[c].astype(F32) for c in range(CHIPS)]
    pair = [piece_of[4 * z] + piece_of[4 * z + 1] for z in range(4)]
    line = [pair[z] + (piece_of[4 * z + 2] + piece_of[4 * z + 3]) for z in range(4)]
    lower = line[0] + line[1]
    for c in range(CHIPS):
        z, x = c // 4, c % 4
        slot = 0
        for bit, value in ((x & 2, pair[z]), (z & 1, line[z - 1]), (z & 2, lower)):
            if bit:
                sb[3 * c + slot] = value.astype(BF)
                slot += 1

    def send_sum(dest, s):
        remote(
            sb.at[3 * dest + s - 1], r2.at[s, chip], two_send, two_recv.at[s], ctx=dest * 2 + core
        ).start()

    for dest in (2, 3):
        @pl.when(chip != dest)
        def _():
            send_sum(dest, 1)

    for s in (1, 2):
        for dx in range(4):
            dest = 4 + x_of[dx]

            @pl.when((x_count[dx] >= s - 1) & (chip != dest))
            def _():
                send_sum(dest, s)

    for s in range(1, 4):
        for dz, dx in ring:
            @pl.when((z_count[dz] + x_count[dx] >= s) & (z_of[dz] > 1))
            def _():
                send_sum(4 * z_of[dz] + x_of[dx], s)

    for n in range(2):
        core_copy(2 * (1 - core) + n).wait_recv()
    core_on = core.astype(F32)
    def core_level(r):
        rows = pl.ds(r * SPAN, SPAN)
        def body(n, carry):
            mixed[n, rows, :] = mixed[n, rows, :] + weighted(dot(q[rows, :], tpeer[n]) * core_on, n, rows, 3)
            return carry

        lax.fori_loop(0, 4, body, 0)

    core_level(0)

    def swap(s):
        return remote(r2.at[s], r2o.at[s], swap_send.at[s], swap_recv.at[s], ctx=other)

    slots = [4 * (1 - bits[0])]
    rank = 1
    for i in range(1, 4):
        slots.append(bits[i] * rank + (1 - bits[i]) * 4)
        rank = rank + bits[i]

    def far_level(r, n, m, source, i):
        rows = pl.ds(r * SPAN, SPAN)
        bucket = source[slots[i], m * 8 : m * 8 + 8].reshape(128, TILE)
        return weighted(dot(q[rows, :], bucket), n, rows, 4 + i)

    def close(r, n, x):
        rows = pl.ds(r * SPAN, SPAN)
        for h in range(2):
            one = x[:, h * DH : (h + 1) * DH]
            one = one * lax.rsqrt(jnp.mean(one * one, axis=-1, keepdims=True) + EPS)
            one = one * gain[2 * n + h]
            hid[rows, pl.ds(pl.multiple_of(n * TILE + h * DH, DH), DH)] = one.astype(BF)

    first_rows = pl.ds(0, SPAN)
    for load in ow_loads:
        load.wait()

    def half_share(n, half):
        depth = pl.ds(pl.multiple_of(half * (WIDTH // 2), WIDTH // 2), WIDTH // 2)
        return dot(hid[first_rows, depth], owv[opposite * 4 + n, depth, :])

    def own_level(i):
        @pl.when(bits[i] == 1)
        def _():
            if i == 0:
                pair_copy.wait_recv()
            else:
                r2[slots[i], chip] = sb[3 * chip + slots[i] - 1]
                here = r2.at[slots[i], others]
                remote(here, here, two_send, two_recv.at[slots[i]], ctx=other).wait_recv()
            swap(slots[i]).start()
            for m in range(2):
                n = 2 * core + m
                mixed[n, first_rows, :] = mixed[n, first_rows, :] + far_level(0, n, m, r2, i)

    def other_level(i):
        @pl.when(bits[i] == 1)
        def _():
            swap(slots[i]).wait_recv()
            for m in range(2):
                n = 2 - 2 * core + m
                mixed[n, first_rows, :] = mixed[n, first_rows, :] + far_level(0, n, m, r2o, i)

    for i in range(4):
        own_level(i)
    for m in range(2):
        close(0, 2 * core + m, mixed[2 * core + m, first_rows, :])
    for n in range(4):
        acc[0, n] = half_share(n, core)
    for i in range(4):
        other_level(i)
    for m in range(2):
        close(0, 2 - 2 * core + m, mixed[2 - 2 * core + m, first_rows, :])
    def far(r):
        core_level(r)
        rows = pl.ds(r * SPAN, SPAN)

        def body(m, carry):
            for n, source in ((2 * core + m, r2), (2 - 2 * core + m, r2o)):
                x = mixed[n, rows, :]
                for i in range(4):
                    bucket = source[slots[i], pl.ds(pl.multiple_of(m * 8, 8), 8)].reshape(128, TILE)
                    x += weighted(dot(q[rows, :], bucket), n, rows, 4 + i)
                close(r, n, x)
            return carry

        lax.fori_loop(0, 2, body, 0)

    def end_near():
        query = acc[1, 4, :, :DK] + dot(full[opposite, end_rows, :], wv[4, end_where, :DK])
        q[end_rows, :] = unit_rows(query).astype(BF)
        scores = score_of(3)

        def last_near(n, carry):
            near(3, n, scores, last[n])
            return carry

        lax.fori_loop(0, 4, last_near, 0)

    def opp_copy(r, d):
        return remote(popp.at[r, d], rpopp.at[r, d], opp_send.at[d, r], opp_recv.at[d, r], head=peers[d])

    def plain_copy(r, d):
        half = pl.ds(2 - 2 * d, 2)
        return remote(psum.at[r, d, half], rpsum.at[r, d, half], plain_send.at[d, r], plain_recv.at[d, r], head=peers[d])

    def sum_copy(r, d):
        half = pl.ds(2 * d, 2)
        return remote(psum.at[r, d, half], rpsum.at[r, d, half], sum_send.at[d, r], sum_recv.at[d, r], head=peers[d])

    def project(r, dest, n):
        return dot(hid[pl.ds(r * SPAN, SPAN), :], owv[dest * 4 + n])

    def opposite_part(r):
        for m in range(2):
            for d in range(2):
                n = 2 * d + m
                share = acc[0, n] + half_share(n, 1 - core) if r == 0 else project(r, opposite, n)
                popp[r, d, m] = share.astype(BF)
                remote(
                    popp.at[r, d, m], rpopp.at[r, d, m], opp_send.at[d, r], opp_recv.at[d, r], head=peers[d]
                ).start()

    def neighbour_part(r):
        for d in range(2):
            def body(n, carry):
                psum[r, d, n] = project(r, peers[d], n).astype(BF)
                return carry

            lax.fori_loop(0, 4, body, 0)
            plain_copy(r, d).start()

    def relay(r):
        for d in range(2):
            opp_copy(r, d).wait_recv()
            for m in range(2):
                n = 2 * d + m
                psum[r, d, n] = (psum[r, d, n].astype(F32) + rpopp[r, d, m].astype(F32)).astype(BF)
            sum_copy(r, d).start()

    def own_part(r):
        def body(n, carry):
            pown[r, n] = project(r, me, n).astype(BF)
            return carry

        lax.fori_loop(0, 4, body, 0)

    def finish(r):
        for d in range(2):
            plain_copy(r, d).wait_recv()
            sum_copy(r, d).wait_recv()
        for n in range(4):
            total = pown[r, n].astype(F32) + rpsum[r, 0, n].astype(F32) + rpsum[r, 1, n].astype(F32)
            out[pl.ds(r * SPAN, SPAN), n * TILE : (n + 1) * TILE] = total.astype(BF)

    for r in range(CHUNKS):
        opposite_part(r)
        neighbour_part(r)
        if r > 0:
            own_part(r - 1)
        if r == 1:
            end_near()
        if r + 1 < CHUNKS:
            far(r + 1)
        relay(r)
        if r > 1:
            finish(r - 2)
    own_part(CHUNKS - 1)
    finish(CHUNKS - 2)

    for r in range(CHUNKS):
        for d in range(2):
            own(r, d).wait_send()
            forward(r, d).wait_send()
            opp_copy(r, d).wait_send()
            plain_copy(r, d).wait_send()
            if r < CHUNKS - 1:
                sum_copy(r, d).wait_send()
    for n in range(4):
        core_copy(n).wait_send()
    remote(cb.at[others], r1.at[others], one_sem.at[0], one_sem.at[1], ctx=other).wait_send()

    @pl.when(bits[0] == 0)
    def _():
        pair_copy.wait_send()

    @pl.when(bits[0] == 1)
    def _():
        swap(0).wait_send()

    for j in range(4):
        @pl.when(count == j)
        def _():
            sent = sb.at[pl.ds(0, 24 - j)]
            remote(sent, sent, two_send, two_recv.at[1], ctx=other).wait_send()
            for s in range(1, j + 1):
                swap(s).wait_send()

    finish(CHUNKS - 1)
    for d in range(2):
        sum_copy(CHUNKS - 1, d).wait_send()


def local(tokens, pair_weight, value_weight, output_weight, level_index, level_table, out_gain):
    any_space = pl.BlockSpec(memory_space=pl.ANY)
    vmem = pl.BlockSpec(memory_space=pltpu.VMEM)
    rows = tokens.shape[0]
    dma = pltpu.SemaphoreType.DMA
    return pl.pallas_call(
        kernel,
        out_shape=pltpu.VMEM((rows, WIDTH), BF),
        in_specs=[any_space] * 7,
        out_specs=vmem,
        scratch_shapes=[
            pltpu.VMEM((8, rows), jnp.int32),
            pltpu.VMEM((64, 16), F32),
            pltpu.VMEM((8, 1, DH), F32),
            pltpu.VMEM((4, rows, WIDTH), BF),
            pltpu.VMEM((5, 4 * WIDTH, TILE), BF),
            pltpu.VMEM((16, WIDTH, TILE), BF),
            pltpu.VMEM((2, 5, SPAN, TILE), F32),
            pltpu.VMEM((4, rows, 128), F32),
            pltpu.VMEM((rows, DK), BF),
            pltpu.VMEM((DK, SPAN), BF),
            pltpu.VMEM((4, SPAN, TILE), BF),
            pltpu.VMEM((4, DK, TILE), F32),
            pltpu.VMEM((4, DK, TILE), BF),
            pltpu.VMEM((4, DK, TILE), BF),
            pltpu.VMEM((4, DK, TILE), F32),
            pltpu.VMEM((4, DK, TILE), BF),
            pltpu.VMEM((4, DK, TILE), BF),
            pltpu.VMEM((4, rows, TILE), F32),
            pltpu.VMEM((CHIPS, 16, TILE), BF),
            pltpu.VMEM((CHIPS, 16, TILE), BF),
            pltpu.VMEM((3 * CHIPS, 16, TILE), BF),
            pltpu.VMEM((5, CHIPS, 16, TILE), BF),
            pltpu.VMEM((5, CHIPS, 16, TILE), BF),
            pltpu.VMEM((rows, WIDTH), BF),
            pltpu.VMEM((CHUNKS, 2, 2, SPAN, TILE), BF),
            pltpu.VMEM((CHUNKS, 2, 2, SPAN, TILE), BF),
            pltpu.VMEM((CHUNKS, 2, 4, SPAN, TILE), BF),
            pltpu.VMEM((CHUNKS, 2, 4, SPAN, TILE), BF),
            pltpu.VMEM((CHUNKS, 4, SPAN, TILE), BF),
            dma((25,)),
            dma((2, CHUNKS)),
            dma((2, CHUNKS)),
            dma((2, CHUNKS)),
            dma((2, CHUNKS)),
            dma((4,)),
            dma((4,)),
            dma((2,)),
            dma((2,)),
            dma(()),
            dma((4,)),
            dma((4,)),
            dma((4,)),
            dma((2, CHUNKS)),
            dma((2, CHUNKS)),
            dma((2, CHUNKS)),
            dma((2, CHUNKS)),
            dma((2, CHUNKS)),
            dma((2, CHUNKS)),
        ],
        compiler_params=pltpu.CompilerParams(
            collective_id=0, has_side_effects=True, vmem_limit_bytes=56 * 1024 * 1024
        ),
        name="layer",
    )(
        tokens, pair_weight, value_weight, output_weight, level_index.T,
        level_table.transpose(0, 2, 1).reshape(64, 16), out_gain.reshape(8, 1, 128),
    )


def solution(mesh):
    return jax.shard_map(
        local,
        mesh=mesh,
        in_specs=(
            P("ctx", "head"),
            P(),
            P(None, "head"),
            P("head", None),
            P("ctx", None),
            P(None, None, "head"),
            P("head"),
        ),
        out_specs=P("ctx", "head"),
        check_vma=False,
    )
```

```python
import math

import jax
import jax.numpy as jnp
from jax import lax
from jax.experimental import pallas as pl
from jax.experimental.pallas import tpu as pltpu
from jax.sharding import PartitionSpec as P

DH = 128
DK = 128
SPAN = 128
EPS = 1e-06
CHUNKS = 4
WIDTH = 1024
TILE = 256
CHIPS = 16
MESH = pl.DeviceIdType.MESH
BF = jnp.bfloat16
F32 = jnp.float32


def dot(a, b):
    return jnp.dot(a, b, preferred_element_type=F32)


def unit_rows(values):
    scale = lax.rsqrt(jnp.mean(values * values, axis=-1, keepdims=True) + EPS)
    return values * scale / math.sqrt(values.shape[-1])


def kernel(
    tok, pw, vw, ow, lidx_in, ltab_in, gain_in, out,
    lidx, ltab, gain,
    full, wv, owv, acc, mixn, q, kt, last, s01, s0b, s2b, tot, tb, tpeer, mixed,
    cb, r1, sb, r2, r2o, hid, popp, rpopp, psum, rpsum, pown,
    w_sem, own_send, own_recv, fwd_send, fwd_recv, core_send, core_recv, one_sem, pair_sem, two_send, two_recv,
    swap_send, swap_recv,
    opp_send, opp_recv, plain_send, plain_recv, sum_send, sum_recv,
):
    me = lax.axis_index("head")
    ctx = lax.axis_index("ctx")
    right = lax.rem(me + 1, 4)
    left = lax.rem(me + 3, 4)
    opposite = lax.rem(me + 2, 4)
    core = lax.rem(ctx, 2)
    chip = lax.div(ctx, 2)
    other = ctx + 1 - 2 * core
    bits = [lax.rem(lax.div(chip, 1 << i), 2) for i in range(4)]
    count = bits[1] + bits[2] + bits[3]
    z_of = [lax.rem(lax.div(chip, 4) + d, 4) for d in range(4)]
    x_of = [lax.rem(lax.rem(chip, 4) + d, 4) for d in range(4)]
    z_count = [lax.rem(z, 2) + lax.div(z, 2) for z in z_of]
    x_count = [lax.div(x, 2) for x in x_of]
    ring = [(dz, dx) for dz in range(4) for dx in range(4) if dz or dx]

    def remote(src, dst, send, recv, **axes):
        return pltpu.make_async_remote_copy(
            src_ref=src, dst_ref=dst, send_sem=send, recv_sem=recv,
            device_id=axes, device_id_type=MESH,
        )

    loads = [
        pltpu.make_async_copy(pw, wv.at[4], w_sem.at[4]),
    ]
    for n in range(4):
        loads.append(pltpu.make_async_copy(vw.at[:, pl.ds(n * TILE, TILE)], wv.at[n], w_sem.at[n]))
    tok_load = pltpu.make_async_copy(tok, full.at[me], w_sem.at[5])
    ow_loads = [
        pltpu.make_async_copy(ow.at[:, pl.ds(t * TILE, TILE)], owv.at[t], w_sem.at[6 + t])
        for t in range(16)
    ]

    barrier = pltpu.get_barrier_semaphore()
    for peer in (left, right):
        pl.semaphore_signal(barrier, inc=1, device_id={"head": peer}, device_id_type=MESH)
    pl.semaphore_signal(barrier, inc=1, device_id={"ctx": other}, device_id_type=MESH)

    for dz, dx in sorted(ring, key=lambda step: (2, 1, 3, 0).index(step[0])):
        dest = (4 * z_of[dz] + x_of[dx]) * 2 + core
        pl.semaphore_signal(barrier, inc=1, device_id={"ctx": dest}, device_id_type=MESH)
    small = [
        pltpu.make_async_copy(src, dst, w_sem.at[22 + i])
        for i, (src, dst) in enumerate(((lidx_in, lidx), (ltab_in, ltab), (gain_in, gain)))
    ]
    for load in small:
        load.start()
    tok_load.start()
    for load in loads:
        load.start()
    pl.semaphore_wait(barrier, 3 + CHIPS - 1)

    peers = (right, left)
    HALF = SPAN // 2

    def own(r, d):
        rows = pl.ds(r * SPAN, SPAN)
        return remote(tok.at[rows], full.at[me, rows], own_send.at[d, r], own_recv.at[d, r], head=peers[d])

    def own_in(r, d):
        rows = pl.ds(r * SPAN, SPAN)
        slot = (left, right)[d]
        return remote(tok.at[rows], full.at[slot, rows], own_send.at[d, r], own_recv.at[d, r], head=peers[d])

    def forward(r, d):
        rows = pl.ds(r * SPAN + d * HALF, HALF)
        slot = (left, right)[d]
        return remote(full.at[slot, rows], full.at[slot, rows], fwd_send.at[d, r], fwd_recv.at[d, r], head=peers[d])

    def forward_in(r, d):
        rows = pl.ds(r * SPAN + d * HALF, HALF)
        return remote(full.at[opposite, rows], full.at[opposite, rows], fwd_send.at[d, r], fwd_recv.at[d, r], head=peers[d])

    for r in range(2):
        for d in range(2):
            own(r, d).start()

    for load in small:
        load.wait()
    row = lax.broadcasted_iota(jnp.int32, (128, 8), 0)
    spread = jnp.where(row // 16 == lax.broadcasted_iota(jnp.int32, (128, 8), 1), 1.0, 0.0).astype(BF)
    wanted = dot(spread, lidx[...].astype(F32).astype(BF))
    entry = lax.broadcasted_iota(jnp.int32, (128, CHUNKS * SPAN), 0) % 16
    onehot = jnp.where(wanted == entry.astype(F32), 1.0, 0.0).T
    exact = lax.Precision.HIGHEST
    level_of = lax.broadcasted_iota(jnp.int32, (64, 128), 0) // 8
    lane_level = lax.broadcasted_iota(jnp.int32, (64, 128), 1) // 16
    placed = jnp.where(level_of == lane_level, jnp.concatenate([ltab[...]] * 8, axis=1), 0.0)
    column = lax.broadcasted_iota(jnp.int32, (128, 64), 0)
    source = lax.broadcasted_iota(jnp.int32, (128, 64), 1)
    for n in range(4):
        take = jnp.where((column < 16) & (source == (column // 2) * 8 + 2 * n + column % 2), 1.0, 0.0)
        table = jnp.dot(take, placed, preferred_element_type=F32, precision=exact).T
        mixn[n] = jnp.dot(onehot, table, preferred_element_type=F32, precision=exact)
    r2[4] = jnp.zeros((CHIPS, 16, TILE), BF)
    r2o[4] = jnp.zeros((CHIPS, 16, TILE), BF)

    def weighted(value, n, rows, level):
        parts = []
        for h in range(2):
            w = mixn[n, rows, 2 * level + h : 2 * level + h + 1]
            parts.append(value[:, h * DH : (h + 1) * DH] * w)
        return jnp.concatenate(parts, axis=1)

    for load in loads:
        load.wait()
    tok_load.wait()
    for load in ow_loads:
        load.start()

    def first_part(r):
        rows = pl.ds(r * SPAN, SPAN)

        def body(n, carry):
            total = None
            for slot in (me, left, right):
                term = dot(full[slot, rows, :], wv[n, pl.ds(pl.multiple_of(slot * WIDTH, WIDTH), WIDTH), :])
                total = term if total is None else total + term
            acc[r % 2, n] = total
            return carry

        lax.fori_loop(0, 5, body, 0)

    def heads_of(r):
        where = pl.ds(pl.multiple_of(opposite * WIDTH, WIDTH), WIDTH)
        rows = pl.ds(r * SPAN, SPAN)
        paired = acc[r % 2, 4] + dot(full[opposite, rows, :], wv[4, where, :])
        q[rows, :] = unit_rows(paired[:, :DK]).astype(BF)
        kt[...] = unit_rows(paired[:, DK:]).T.astype(BF)

    def value_of(r, n):
        where = pl.ds(pl.multiple_of(opposite * WIDTH, WIDTH), WIDTH)
        rows = pl.ds(r * SPAN, SPAN)
        return (acc[r % 2, n] + dot(full[opposite, rows, :], wv[n, where, :])).astype(BF)

    def score_of(r):
        scores = dot(q[pl.ds(r * SPAN, SPAN), :], kt[...])
        t = lax.broadcasted_iota(jnp.int32, (SPAN, SPAN), 0)
        s = lax.broadcasted_iota(jnp.int32, (SPAN, SPAN), 1)
        return jnp.where(t >= s, scores, 0.0).astype(BF)

    def near(r, n, scores, value):
        rows = pl.ds(r * SPAN, SPAN)
        query = q[rows, :]
        result = weighted(dot(scores, value), n, rows, 0)
        if r == 1:
            result += weighted(dot(query, s0b[n]), n, rows, 1)
        if r == 3:
            result += weighted(dot(query, s2b[n]), n, rows, 1)
        if r >= 2:
            result += weighted(dot(query, s01[n].astype(BF)), n, rows, 2)
        mixed[n, rows, :] = result

    def second_part(r):
        heads_of(r)
        scores = score_of(r)

        def body(n, carry):
            value = value_of(r, n)
            near(r, n, scores, value)
            state = dot(kt[...], value)
            if r == 0:
                s01[n] = state
                s0b[n] = state.astype(BF)
            elif r == 1:
                s01[n] = s01[n] + state
            else:
                s2b[n] = state.astype(BF)
                tot[n] = s01[n] + state
            return carry

        lax.fori_loop(0, 4, body, 0)

    for r in range(CHUNKS):
        for d in range(2):
            own_in(r, d).wait_recv()
            forward(r, d).start()
        if r + 2 < CHUNKS:
            for d in range(2):
                own(r + 2, d).start()
        first_part(r)
        if r > 0:
            for d in range(2):
                forward_in(r - 1, d).wait_recv()
            second_part(r - 1)
    for d in range(2):
        forward_in(CHUNKS - 1, d).wait_recv()

    def core_copy(n):
        return remote(tb.at[n], tpeer.at[n], core_send.at[n], core_recv.at[n], ctx=other)

    def piece(dest):
        return remote(cb.at[dest], r1.at[chip], one_sem.at[0], one_sem.at[1], ctx=dest * 2 + core)

    end_rows = pl.ds(3 * SPAN, SPAN)
    end_where = pl.ds(pl.multiple_of(opposite * WIDTH, WIDTH), WIDTH)
    key = acc[1, 4, :, DK:] + dot(full[opposite, end_rows, :], wv[4, end_where, DK:])
    values = []
    for order in range(4):
        values.append(value_of(3, lax.rem(2 * (1 - core) + order, 4)))
    key_t = unit_rows(key).T.astype(BF)
    kt[...] = key_t
    for order in range(4):
        n = lax.rem(2 * (1 - core) + order, 4)
        last[n] = values[order]
        total = tot[n] + dot(key_t, values[order])
        tot[n] = total
        tb[n] = total.astype(BF)
        core_copy(n).start()
        if order >= 2:
            m = order - 2
            core_copy(n).wait_recv()
            both = tot[n] + tpeer[n].astype(F32)
            cb[m * 8 : (m + 1) * 8] = both.astype(BF).reshape(8, 16, TILE)

            for dz in range(2):
                z = 2 * m + lax.rem(z_of[0] + dz, 2)
                for dx in range(4):
                    dest = 4 * z + x_of[dx]
                    if dx:
                        piece(dest).start()
                    else:
                        @pl.when(dest != chip)
                        def _():
                            piece(dest).start()

    pair_copy = remote(cb, r2.at[0], pair_sem.at[0], pair_sem.at[1], ctx=lax.rem(ctx + 2, 32))

    @pl.when(bits[0] == 0)
    def _():
        pair_copy.start()

    r1[chip] = cb[chip]
    others = pl.ds(0, CHIPS - 1)
    remote(cb.at[others], r1.at[others], one_sem.at[0], one_sem.at[1], ctx=other).wait_recv()

    piece_of = [r1[c].astype(F32) for c in range(CHIPS)]
    pair = [piece_of[4 * z] + piece_of[4 * z + 1] for z in range(4)]
    line = [pair[z] + (piece_of[4 * z + 2] + piece_of[4 * z + 3]) for z in range(4)]
    lower = line[0] + line[1]
    for c in range(CHIPS):
        z, x = c // 4, c % 4
        slot = 0
        for bit, value in ((x & 2, pair[z]), (z & 1, line[z - 1]), (z & 2, lower)):
            if bit:
                sb[3 * c + slot] = value.astype(BF)
                slot += 1

    def send_sum(dest, s):
        remote(
            sb.at[3 * dest + s - 1], r2.at[s, chip], two_send, two_recv.at[s], ctx=dest * 2 + core
        ).start()

    for dest in (2, 3):
        @pl.when(chip != dest)
        def _():
            send_sum(dest, 1)

    for s in (1, 2):
        for dx in range(4):
            dest = 4 + x_of[dx]

            @pl.when((x_count[dx] >= s - 1) & (chip != dest))
            def _():
                send_sum(dest, s)

    for s in range(1, 4):
        for dz, dx in ring:
            @pl.when((z_count[dz] + x_count[dx] >= s) & (z_of[dz] > 1))
            def _():
                send_sum(4 * z_of[dz] + x_of[dx], s)

    for n in range(2):
        core_copy(2 * (1 - core) + n).wait_recv()
    core_on = core.astype(F32)
    def core_level(r):
        rows = pl.ds(r * SPAN, SPAN)
        def body(n, carry):
            mixed[n, rows, :] = mixed[n, rows, :] + weighted(dot(q[rows, :], tpeer[n]) * core_on, n, rows, 3)
            return carry

        lax.fori_loop(0, 4, body, 0)

    core_level(0)

    def swap(s):
        return remote(r2.at[s], r2o.at[s], swap_send.at[s], swap_recv.at[s], ctx=other)

    slots = [4 * (1 - bits[0])]
    rank = 1
    for i in range(1, 4):
        slots.append(bits[i] * rank + (1 - bits[i]) * 4)
        rank = rank + bits[i]

    def far_level(r, n, m, source, i):
        rows = pl.ds(r * SPAN, SPAN)
        bucket = source[slots[i], m * 8 : m * 8 + 8].reshape(128, TILE)
        return weighted(dot(q[rows, :], bucket), n, rows, 4 + i)

    def close(r, n, x):
        rows = pl.ds(r * SPAN, SPAN)
        for h in range(2):
            one = x[:, h * DH : (h + 1) * DH]
            one = one * lax.rsqrt(jnp.mean(one * one, axis=-1, keepdims=True) + EPS)
            one = one * gain[2 * n + h]
            hid[rows, pl.ds(pl.multiple_of(n * TILE + h * DH, DH), DH)] = one.astype(BF)

    first_rows = pl.ds(0, SPAN)
    for load in ow_loads:
        load.wait()

    def half_share(n, half):
        depth = pl.ds(pl.multiple_of(half * (WIDTH // 2), WIDTH // 2), WIDTH // 2)
        return dot(hid[first_rows, depth], owv[opposite * 4 + n, depth, :])

    def own_level(i):
        @pl.when(bits[i] == 1)
        def _():
            if i == 0:
                pair_copy.wait_recv()
            else:
                r2[slots[i], chip] = sb[3 * chip + slots[i] - 1]
                here = r2.at[slots[i], others]
                remote(here, here, two_send, two_recv.at[slots[i]], ctx=other).wait_recv()
            swap(slots[i]).start()
            for m in range(2):
                n = 2 * core + m
                mixed[n, first_rows, :] = mixed[n, first_rows, :] + far_level(0, n, m, r2, i)

    def other_level(i):
        @pl.when(bits[i] == 1)
        def _():
            swap(slots[i]).wait_recv()
            for m in range(2):
                n = 2 - 2 * core + m
                mixed[n, first_rows, :] = mixed[n, first_rows, :] + far_level(0, n, m, r2o, i)

    for i in range(4):
        own_level(i)
    for m in range(2):
        close(0, 2 * core + m, mixed[2 * core + m, first_rows, :])
    for n in range(4):
        acc[0, n] = half_share(n, core)
    for i in range(4):
        other_level(i)
    for m in range(2):
        close(0, 2 - 2 * core + m, mixed[2 - 2 * core + m, first_rows, :])
    def far(r):
        core_level(r)
        rows = pl.ds(r * SPAN, SPAN)

        def body(m, carry):
            for n, source in ((2 * core + m, r2), (2 - 2 * core + m, r2o)):
                x = mixed[n, rows, :]
                for i in range(4):
                    bucket = source[slots[i], pl.ds(pl.multiple_of(m * 8, 8), 8)].reshape(128, TILE)
                    x += weighted(dot(q[rows, :], bucket), n, rows, 4 + i)
                close(r, n, x)
            return carry

        lax.fori_loop(0, 2, body, 0)

    def end_near():
        query = acc[1, 4, :, :DK] + dot(full[opposite, end_rows, :], wv[4, end_where, :DK])
        q[end_rows, :] = unit_rows(query).astype(BF)
        scores = score_of(3)

        def last_near(n, carry):
            near(3, n, scores, last[n])
            return carry

        lax.fori_loop(0, 4, last_near, 0)

    def opp_copy(r, d):
        return remote(popp.at[r, d], rpopp.at[r, d], opp_send.at[d, r], opp_recv.at[d, r], head=peers[d])

    def plain_copy(r, d):
        half = pl.ds(2 - 2 * d, 2)
        return remote(psum.at[r, d, half], rpsum.at[r, d, half], plain_send.at[d, r], plain_recv.at[d, r], head=peers[d])

    def sum_copy(r, d):
        half = pl.ds(2 * d, 2)
        return remote(psum.at[r, d, half], rpsum.at[r, d, half], sum_send.at[d, r], sum_recv.at[d, r], head=peers[d])

    def project(r, dest, n):
        return dot(hid[pl.ds(r * SPAN, SPAN), :], owv[dest * 4 + n])

    def opposite_part(r):
        for m in range(2):
            for d in range(2):
                n = 2 * d + m
                share = acc[0, n] + half_share(n, 1 - core) if r == 0 else project(r, opposite, n)
                popp[r, d, m] = share.astype(BF)
                remote(
                    popp.at[r, d, m], rpopp.at[r, d, m], opp_send.at[d, r], opp_recv.at[d, r], head=peers[d]
                ).start()

    def neighbour_part(r):
        for d in range(2):
            def body(n, carry):
                psum[r, d, n] = project(r, peers[d], n).astype(BF)
                return carry

            lax.fori_loop(0, 4, body, 0)
            plain_copy(r, d).start()

    def relay(r):
        for d in range(2):
            opp_copy(r, d).wait_recv()
            for m in range(2):
                n = 2 * d + m
                psum[r, d, n] = (psum[r, d, n].astype(F32) + rpopp[r, d, m].astype(F32)).astype(BF)
                remote(
                    psum.at[r, d, n], rpsum.at[r, d, n], sum_send.at[d, r], sum_recv.at[d, r], head=peers[d]
                ).start()

    def own_part(r):
        def body(n, carry):
            pown[r, n] = project(r, me, n).astype(BF)
            return carry

        lax.fori_loop(0, 4, body, 0)

    def finish(r):
        for d in range(2):
            plain_copy(r, d).wait_recv()
            sum_copy(r, d).wait_recv()
        for n in range(4):
            total = pown[r, n].astype(F32) + rpsum[r, 0, n].astype(F32) + rpsum[r, 1, n].astype(F32)
            out[pl.ds(r * SPAN, SPAN), n * TILE : (n + 1) * TILE] = total.astype(BF)

    for r in range(CHUNKS):
        opposite_part(r)
        neighbour_part(r)
        if r > 0:
            own_part(r - 1)
        if r == 1:
            end_near()
        if r + 1 < CHUNKS:
            far(r + 1)
        relay(r)
        if r > 1:
            finish(r - 2)
    own_part(CHUNKS - 1)
    finish(CHUNKS - 2)

    for r in range(CHUNKS):
        for d in range(2):
            own(r, d).wait_send()
            forward(r, d).wait_send()
            opp_copy(r, d).wait_send()
            plain_copy(r, d).wait_send()
            if r < CHUNKS - 1:
                sum_copy(r, d).wait_send()
    for n in range(4):
        core_copy(n).wait_send()
    remote(cb.at[others], r1.at[others], one_sem.at[0], one_sem.at[1], ctx=other).wait_send()

    @pl.when(bits[0] == 0)
    def _():
        pair_copy.wait_send()

    @pl.when(bits[0] == 1)
    def _():
        swap(0).wait_send()

    for j in range(4):
        @pl.when(count == j)
        def _():
            sent = sb.at[pl.ds(0, 24 - j)]
            remote(sent, sent, two_send, two_recv.at[1], ctx=other).wait_send()
            for s in range(1, j + 1):
                swap(s).wait_send()

    finish(CHUNKS - 1)
    for d in range(2):
        sum_copy(CHUNKS - 1, d).wait_send()


def local(tokens, pair_weight, value_weight, output_weight, level_index, level_table, out_gain):
    any_space = pl.BlockSpec(memory_space=pl.ANY)
    vmem = pl.BlockSpec(memory_space=pltpu.VMEM)
    rows = tokens.shape[0]
    dma = pltpu.SemaphoreType.DMA
    return pl.pallas_call(
        kernel,
        out_shape=pltpu.VMEM((rows, WIDTH), BF),
        in_specs=[any_space] * 7,
        out_specs=vmem,
        scratch_shapes=[
            pltpu.VMEM((8, rows), jnp.int32),
            pltpu.VMEM((64, 16), F32),
            pltpu.VMEM((8, 1, DH), F32),
            pltpu.VMEM((4, rows, WIDTH), BF),
            pltpu.VMEM((5, 4 * WIDTH, TILE), BF),
            pltpu.VMEM((16, WIDTH, TILE), BF),
            pltpu.VMEM((2, 5, SPAN, TILE), F32),
            pltpu.VMEM((4, rows, 128), F32),
            pltpu.VMEM((rows, DK), BF),
            pltpu.VMEM((DK, SPAN), BF),
            pltpu.VMEM((4, SPAN, TILE), BF),
            pltpu.VMEM((4, DK, TILE), F32),
            pltpu.VMEM((4, DK, TILE), BF),
            pltpu.VMEM((4, DK, TILE), BF),
            pltpu.VMEM((4, DK, TILE), F32),
            pltpu.VMEM((4, DK, TILE), BF),
            pltpu.VMEM((4, DK, TILE), BF),
            pltpu.VMEM((4, rows, TILE), F32),
            pltpu.VMEM((CHIPS, 16, TILE), BF),
            pltpu.VMEM((CHIPS, 16, TILE), BF),
            pltpu.VMEM((3 * CHIPS, 16, TILE), BF),
            pltpu.VMEM((5, CHIPS, 16, TILE), BF),
            pltpu.VMEM((5, CHIPS, 16, TILE), BF),
            pltpu.VMEM((rows, WIDTH), BF),
            pltpu.VMEM((CHUNKS, 2, 2, SPAN, TILE), BF),
            pltpu.VMEM((CHUNKS, 2, 2, SPAN, TILE), BF),
            pltpu.VMEM((CHUNKS, 2, 4, SPAN, TILE), BF),
            pltpu.VMEM((CHUNKS, 2, 4, SPAN, TILE), BF),
            pltpu.VMEM((CHUNKS, 4, SPAN, TILE), BF),
            dma((25,)),
            dma((2, CHUNKS)),
            dma((2, CHUNKS)),
            dma((2, CHUNKS)),
            dma((2, CHUNKS)),
            dma((4,)),
            dma((4,)),
            dma((2,)),
            dma((2,)),
            dma(()),
            dma((4,)),
            dma((4,)),
            dma((4,)),
            dma((2, CHUNKS)),
            dma((2, CHUNKS)),
            dma((2, CHUNKS)),
            dma((2, CHUNKS)),
            dma((2, CHUNKS)),
            dma((2, CHUNKS)),
        ],
        compiler_params=pltpu.CompilerParams(
            collective_id=0, has_side_effects=True, vmem_limit_bytes=56 * 1024 * 1024
        ),
        name="layer",
    )(
        tokens, pair_weight, value_weight, output_weight, level_index.T,
        level_table.transpose(0, 2, 1).reshape(64, 16), out_gain.reshape(8, 1, 128),
    )


def solution(mesh):
    return jax.shard_map(
        local,
        mesh=mesh,
        in_specs=(
            P("ctx", "head"),
            P(),
            P(None, "head"),
            P("head", None),
            P("ctx", None),
            P(None, None, "head"),
            P("head"),
        ),
        out_specs=P("ctx", "head"),
        check_vma=False,
    )
```
